32 devices in a mesh: mem: 4 (over y, x), tile: 4 (over z), grp: 2 (over core).
Axes of the slice: x: 2, y: 2, z: 4, core: 2. Of those that a mesh axis runs over, the one named last changes fastest.
Arguments:
- members: float32 [3, 128, 64, 512], P(None, 'mem', ('tile', 'grp')), may hold values from -0.6 to 0.6
- obs_cells: int32 [8, 4, 1024], P(('tile', 'grp'), 'mem'), may hold values from 0 to 1023
- obs_count: int32 [8, 4], P(('tile', 'grp'), 'mem'), may hold values from 128 to 1024, as said below
- obs_values: float32 [8, 4, 1024], P(('tile', 'grp'), 'mem'), may hold values from -0.6 to 0.6
- obs_error: float32 [8, 4, 1024], P(('tile', 'grp'), 'mem'), may hold values from 0.03 to 0.3
- obs_noise: float32 [8, 4, 1024, 128], P(('tile', 'grp'), 'mem'), may hold values from -6 to 6
Outputs:
- analysis: bfloat16 [3, 128, 64, 512], P(None, None, ('tile', 'grp'), 'mem')
The draws below stay inside these ranges and needn't reach their ends.
Inputs may be any that keep to these rules, and one draw needn't show every extreme that they name: `obs_count`: a multiple of 128; some tile has exactly 1024 live slots in every draw.
All inputs are finite; a program needn't handle non-finite values.
Results may differ from the reference program's by a relative error of at most 0.0058.
Values may be sent and summed in bfloat16 or wider, within the bound.
A program may use at most 64 MiB of HBM per device.

```python
import math
import jax
import jax.numpy as jnp
from jax import lax

STRIP_LINES = 8
DOMAIN_VERTICALS = 512
STEPS = 4
OBS_CAP = 1024
REALIZATION_NUM = 128
DOMAIN_LINES = 64
PATCHES_SOUTHWARD = 8
PATCHES_EASTWARD = 4
PATCH_BREADTH = 128
PATCH_POINTS = 1024


def draw_obs_count(key, part):
    key_one, key_two, key_three = jax.random.split(jax.random.fold_in(key, 17), 3)
    blocks_most = OBS_CAP // 128
    factor_one = jax.random.randint(key_one, (PATCHES_SOUTHWARD, PATCHES_EASTWARD), 0, blocks_most)
    factor_two = jax.random.randint(key_two, (PATCHES_SOUTHWARD, PATCHES_EASTWARD), 0, blocks_most)
    block_count = 1 + factor_one * factor_two // (blocks_most - 1)
    position = jax.random.randint(key_three, (), 0, PATCHES_SOUTHWARD * PATCHES_EASTWARD)
    flattened = block_count.reshape(-1).at[position].set(blocks_most)
    return (flattened * 128).reshape(PATCHES_SOUTHWARD, PATCHES_EASTWARD).astype(jnp.int32)


def touch_ends(entries, key, smallest, largest):
    longest = entries.shape.index(max(entries.shape))
    spots = []
    for shift in (0, 1):
        where = [jax.random.randint(jax.random.fold_in(key, axis), (), 0, length) for axis, length in enumerate(entries.shape)]
        where[longest] = (where[longest] + shift) % entries.shape[longest]
        spots.append(tuple(where))
    return entries.at[spots[0]].set(smallest).at[spots[1]].set(largest)


def steps_of(own_key, dims, pieces, smallest, largest):
    def one(dim, parts):
        steps = jax.random.uniform(jax.random.fold_in(jax.random.fold_in(own_key, 6), dim), (parts,), jnp.float32, smallest / len(pieces), largest / len(pieces))
        return jnp.repeat(jnp.exp(steps), dims[dim] // parts).reshape((-1,) + (1,) * (len(dims) - dim - 1))

    gain = one(*pieces[0])
    for cut in pieces[1:]:
        gain = gain * one(*cut)
    return gain


def centred(key, extent, width, most, cuts=(), held_as=jnp.bfloat16):
    factor_of = steps_of(key, extent, cuts, -0.22, 0.18) if cuts else 1.0
    values = jax.random.normal(key, extent, jnp.float32) * width * factor_of
    return jnp.minimum(jnp.maximum(values, -most), most).astype(held_as)


def setup_inputs(seed: int = 0) -> dict:
    seeds = jax.random.split(jax.random.key(seed), 7)
    members = centred(seeds[0], (3, REALIZATION_NUM, DOMAIN_LINES, DOMAIN_VERTICALS), 0.1, 0.6, ((1, 4), (2, 8)), jnp.float32)
    obs_cells = touch_ends(jax.random.randint(seeds[1], (PATCHES_SOUTHWARD, PATCHES_EASTWARD, OBS_CAP), 0, PATCH_POINTS), jax.random.fold_in(seeds[1], 1), 0, PATCH_POINTS - 1).astype(jnp.int32)
    obs_count = draw_obs_count(jax.random.fold_in(seeds[6], 71), 0)
    obs_values = centred(seeds[3], (PATCHES_SOUTHWARD, PATCHES_EASTWARD, OBS_CAP), 0.1, 0.6, ((0, 8), (1, 4)), jnp.float32)
    obs_error = jnp.clip(jnp.exp(math.log(0.3) - 2.3025852 * jax.random.uniform(seeds[4], (PATCHES_SOUTHWARD, PATCHES_EASTWARD, OBS_CAP), jnp.float32) ** steps_of(seeds[4], (PATCHES_SOUTHWARD, PATCHES_EASTWARD, OBS_CAP), ((0, 8), (1, 4)), -0.2, 0.2)), 0.03, 0.3)
    obs_noise = centred(seeds[5], (PATCHES_SOUTHWARD, PATCHES_EASTWARD, OBS_CAP, REALIZATION_NUM), 1.0, 6.0, ((0, 8), (1, 4)), jnp.float32)
    return dict(members=members, obs_cells=obs_cells, obs_count=obs_count, obs_values=obs_values, obs_error=obs_error, obs_noise=obs_noise)


courant = 0.3
gravity = 1.0
coriolis = 0.1

def beside_all(field_e, field_w, field_n, field_s):
    return 0.25 * (field_e + field_w + field_n + field_s)

def advance(padded):
    height = padded[0]
    zonal = padded[1]
    meridional = padded[2]
    height_e, height_w, height_mid = (height[:, 2:, :], height[:, :-2, :], height[:, 1:-1, :])
    zonal_e, zonal_w, zonal_mid = (zonal[:, 2:, :], zonal[:, :-2, :], zonal[:, 1:-1, :])
    merid_e, merid_w, merid_mid = (meridional[:, 2:, :], meridional[:, :-2, :], meridional[:, 1:-1, :])
    height_n, height_s = (jnp.roll(height_mid, -1, axis=2), jnp.roll(height_mid, 1, axis=2))
    zonal_n, zonal_s = (jnp.roll(zonal_mid, -1, axis=2), jnp.roll(zonal_mid, 1, axis=2))
    merid_n, merid_s = (jnp.roll(merid_mid, -1, axis=2), jnp.roll(merid_mid, 1, axis=2))
    new_height = beside_all(height_e, height_w, height_n, height_s) - courant * ((1.0 + height_e) * zonal_e - (1.0 + height_w) * zonal_w) - courant * ((1.0 + height_n) * merid_n - (1.0 + height_s) * merid_s)
    new_zonal = beside_all(zonal_e, zonal_w, zonal_n, zonal_s) - courant * (0.5 * zonal_e * zonal_e + gravity * height_e - (0.5 * zonal_w * zonal_w + gravity * height_w)) - courant * merid_mid * (zonal_n - zonal_s) + coriolis * merid_mid
    new_merid = beside_all(merid_e, merid_w, merid_n, merid_s) - courant * (0.5 * merid_n * merid_n + gravity * height_n - (0.5 * merid_s * merid_s + gravity * height_s)) - courant * zonal_mid * (merid_e - merid_w) - coriolis * zonal_mid
    return jnp.stack([new_height, new_zonal, new_merid])

def predict_realization_group(fluid_condition):
    for step_index in range(STEPS):
        padded = jnp.concatenate([fluid_condition[:, :, -1:, :], fluid_condition, fluid_condition[:, :, :1, :]], axis=2)
        fluid_condition = advance(padded)
    return fluid_condition

def analyse(fields, cell_ids, live_count, obs_vals, obs_std, perturb):
    ens_size = fields.shape[1]
    states = fields.astype(jnp.float32)
    spread = states - jnp.mean(states, axis=1, keepdims=True)
    observed = jnp.take(states[0], cell_ids, axis=1)
    obs_spread = observed - jnp.mean(observed, axis=0, keepdims=True)
    slot_ids = jnp.arange(obs_vals.shape[0], dtype=jnp.int32)
    weights = jnp.where(slot_ids < live_count, 1.0 / (obs_std * obs_std), 0.0).astype(jnp.float32)
    weighted = obs_spread * weights[None, :]
    innov = obs_vals[None, :] + obs_std[None, :] * perturb.T - observed
    gram = (ens_size - 1.0) * jnp.eye(ens_size, dtype=jnp.float32) + jnp.dot(weighted, obs_spread.T, precision=lax.Precision.HIGHEST)
    rhs_matrix = jnp.dot(weighted, innov.T, precision=lax.Precision.HIGHEST)
    factor = jnp.linalg.cholesky(gram)
    weight_matrix = jax.scipy.linalg.cho_solve((factor, True), rhs_matrix)
    update = jnp.einsum('vkc,kj->vjc', spread, weight_matrix, precision=lax.Precision.HIGHEST)
    return (states + update).astype(jnp.bfloat16)

def reference(members, obs_cells, obs_count, obs_values, obs_error, obs_noise):
    batch_size = math.gcd(REALIZATION_NUM, 16)
    realization_groups = jnp.moveaxis(members.reshape(3, REALIZATION_NUM // batch_size, batch_size, DOMAIN_LINES, DOMAIN_VERTICALS), 1, 0)
    advanced_conditions = lax.map(predict_realization_group, realization_groups)
    predict_realizations = jnp.moveaxis(advanced_conditions, 0, 1).reshape(3, REALIZATION_NUM, DOMAIN_LINES, DOMAIN_VERTICALS).astype(jnp.bfloat16)
    condition_patches = predict_realizations.reshape(3, REALIZATION_NUM, PATCHES_SOUTHWARD, STRIP_LINES, PATCHES_EASTWARD, PATCH_BREADTH).transpose(2, 4, 0, 1, 3, 5).reshape(PATCHES_SOUTHWARD * PATCHES_EASTWARD, 3, REALIZATION_NUM, PATCH_POINTS)
    results = lax.map(lambda item: analyse(*item), (condition_patches, obs_cells.reshape(PATCHES_SOUTHWARD * PATCHES_EASTWARD, OBS_CAP), obs_count.reshape(PATCHES_SOUTHWARD * PATCHES_EASTWARD), obs_values.reshape(PATCHES_SOUTHWARD * PATCHES_EASTWARD, OBS_CAP), obs_error.reshape(PATCHES_SOUTHWARD * PATCHES_EASTWARD, OBS_CAP), obs_noise.reshape(PATCHES_SOUTHWARD * PATCHES_EASTWARD, OBS_CAP, REALIZATION_NUM)))
    return results.reshape(PATCHES_SOUTHWARD, PATCHES_EASTWARD, 3, REALIZATION_NUM, STRIP_LINES, PATCH_BREADTH).transpose(2, 3, 0, 4, 1, 5).reshape(3, REALIZATION_NUM, DOMAIN_LINES, DOMAIN_VERTICALS)
```

```python
import jax
import jax.numpy as jnp
from jax import lax
from jax.experimental import pallas as pl
from jax.experimental.pallas import tpu as pltpu
from jax.sharding import PartitionSpec as P

STEPS = 4
NEWTON_STEPS = 13

courant = 0.3
gravity = 1.0
coriolis = 0.1
VMEM_BYTES = 60000000
MESH = pl.DeviceIdType.MESH


def advance(west, mid, east):
    (hw, uw, vw), (h, u, v), (he, ue, ve) = west, mid, east
    cols = h.shape[1]
    north = lambda q: pltpu.roll(q, cols - 1, 1)
    south = lambda q: pltpu.roll(q, 1, 1)
    hn, hs, un, us, vn, vs = north(h), south(h), north(u), south(u), north(v), south(v)
    new_h = (
        0.25 * (he + hw + hn + hs)
        - courant * ((1.0 + he) * ue - (1.0 + hw) * uw)
        - courant * ((1.0 + hn) * vn - (1.0 + hs) * vs)
    )
    new_u = (
        0.25 * (ue + uw + un + us)
        - courant * ((0.5 * ue * ue + gravity * he) - (0.5 * uw * uw + gravity * hw))
        - courant * v * (un - us)
        + coriolis * v
    )
    new_v = (
        0.25 * (ve + vw + vn + vs)
        - courant * ((0.5 * vn * vn + gravity * hn) - (0.5 * vs * vs + gravity * hs))
        - courant * u * (ve - vw)
        - coriolis * u
    )
    return new_h, new_u, new_v


def split(q):
    high = q.astype(jnp.bfloat16)
    rest = q - high.astype(jnp.float32)
    middle = rest.astype(jnp.bfloat16)
    return high, middle, (rest - middle.astype(jnp.float32)).astype(jnp.bfloat16)


def mxu(a, b):
    return jnp.dot(a, b, preferred_element_type=jnp.float32)


def product(a, b):
    (ah, am, al), (bh, bm, bl) = a, b
    size = bh.shape[1]
    top = mxu(
        jnp.concatenate([ah, am], axis=1),
        jnp.concatenate([jnp.concatenate([bh, bm], axis=1)] * 2, axis=0),
    )
    low = mxu(jnp.concatenate([ah, al], axis=1), jnp.concatenate([bl, bh], axis=0))
    return top[:, :size] + (top[:, size:] + low)


def solve_turned(gram, rhs, least):
    size = gram.shape[0]
    bound = jnp.max(jnp.sum(jnp.abs(gram), axis=0, keepdims=True), axis=1, keepdims=True)
    bound = jnp.broadcast_to(bound, (1, size))
    scale = 1.0 / bound
    eye = jnp.where(
        lax.broadcasted_iota(jnp.int32, (size, size), 0) == lax.broadcasted_iota(jnp.int32, (size, size), 1), 1.0, 0.0
    )
    low = least * scale
    y, x = gram * scale, eye * scale
    for _ in range(NEWTON_STEPS):
        mid = 1.0 + low
        gain = 4.0 / (mid * mid)
        low = gain * low
        parts = split(y)
        both = [jnp.concatenate(pair, axis=0) for pair in zip(parts, split(x))]
        done = product(both, parts)
        y = gain * (mid * y - done[:size])
        x = gain * (mid * x - done[size:])
    inverse = split(x)
    found = product(split(rhs), inverse)
    rest = rhs - product(split(found), split(gram))
    return found + product(split(rest), inverse), eye


def neighbour_ids():
    groups = lax.axis_size("grp")
    total = lax.axis_size("tile") * groups
    me = lax.axis_index("tile") * groups + lax.axis_index("grp")
    after, before = lax.rem(me + 1, total), lax.rem(me + total - 1, total)
    return [{"tile": i // groups, "grp": lax.rem(i, groups)} for i in (after, before)]


def kernel(
    members_hbm, count_hbm, cells_hbm, values_hbm, error_hbm, noise_hbm, out_hbm,
    lev, edges, halo, ready, recv, noise, cells, values, error, count, pick, target, observed, tall, packed,
    row_sem, load_sem, halo_send, halo_recv, part_send, part_recv, own_sem, out_sem,
):
    fields, ens, rows, cols = members_hbm.shape
    waves = rows
    assert rows == 2 * STEPS
    lines = rows + 2 * STEPS
    parts, tile_cols = ready.shape[1], ready.shape[4]
    full = parts * ens
    slots = cells.shape[1]
    me = lax.axis_index("mem")
    after, before = neighbour_ids()
    peers = [lax.rem(me + p, parts) for p in range(1, parts)]
    targets = [after, before] + [{"mem": p} for p in peers]
    quick = 1 - lax.rem(lax.axis_index("grp"), 2)

    def row_load(r):
        return pltpu.make_async_copy(members_hbm.at[:, :, r, :], lev.at[STEPS + r], row_sem.at[r])

    small = [
        pltpu.make_async_copy(src, dst, load_sem.at[i])
        for i, (src, dst) in enumerate(
            ((noise_hbm, noise), (cells_hbm, cells), (values_hbm, values), (error_hbm, error), (count_hbm, count))
        )
    ]
    for k in range(STEPS):
        row_load(rows - 1 - k).start()
        row_load(k).start()
    for load in small:
        load.start()
    barrier = pltpu.get_barrier_semaphore()
    for target_id in targets:
        pl.semaphore_signal(barrier, inc=1, device_id=target_id, device_id_type=MESH)

    def halo_copy(way, k):
        return pltpu.make_async_remote_copy(
            src_ref=edges.at[way, k],
            dst_ref=halo.at[way, k],
            send_sem=halo_send.at[way, k],
            recv_sem=halo_recv.at[way, k],
            device_id=(after, before)[way],
            device_id_type=MESH,
        )

    for k in range(STEPS):
        for way, r in ((0, rows - 1 - k), (1, k)):
            row_load(r).wait()
            edges[way, k] = lev[STEPS + r].astype(jnp.bfloat16)
        if k == 0:
            pl.semaphore_wait(barrier, len(targets))
        for way in range(2):
            halo_copy(way, k).start()

    def stencil(base, half):
        def at(i):
            return [lev[i, f, pl.ds(half, 8), :] for f in range(fields)]

        return advance(at(base - 1), at(base), at(base + 1))

    def step_row(level, line):
        base = level * lines + line
        for half in range(0, ens, 8):
            done = stencil(base, half)
            for f in range(fields):
                lev[base + lines, f, pl.ds(half, 8), :] = done[f]

    for level in range(STEPS - 1):

        def inner_row(i, carry, level=level):
            step_row(level, STEPS + level + 1 + i)
            return carry

        lax.fori_loop(0, rows - 2 * (level + 1), inner_row, 0)

    def wave_side(w):
        late = w // STEPS
        return quick + late - 2 * quick * late, lax.rem(w, STEPS)

    def wave_row(w):
        side, k = wave_side(w)
        return (STEPS - 1 - k) + side * (2 * k + 1)

    def part_copy(w, kind, p):
        f, number = ((0, 1), (1, fields - 1))[kind]
        return pltpu.make_async_remote_copy(
            src_ref=ready.at[w, peers[p], pl.ds(f, number)],
            dst_ref=recv.at[w, pl.ds(f, number), pl.ds(me * ens, ens)],
            send_sem=part_send.at[w, kind, p],
            recv_sem=part_recv.at[w, kind, p],
            device_id={"mem": peers[p]},
            device_id_type=MESH,
        )

    def own_copy(w):
        return pltpu.make_async_copy(ready.at[w, me], recv.at[w, :, pl.ds(me * ens, ens)], own_sem.at[w])

    def wave(w, carry):
        side, k = wave_side(w)
        sign = 1 - 2 * side
        start = (STEPS - 1 - k) + side * (2 * k + lines - 2 * STEPS + 1)
        pltpu.make_async_copy(halo.at[side, k], halo.at[side, k], halo_recv.at[side, k]).wait()
        lev[start] = halo[side, k].astype(jnp.float32)

        def up(level, c):
            step_row(level, start + sign * (level + 1))
            return c

        lax.fori_loop(0, STEPS - 1, up, 0)
        base = (STEPS - 1) * lines + start + sign * STEPS
        for m in range(0, ens, 16):
            pair = [stencil(base, m), stencil(base, m + 8)]
            for f in range(fields):
                both = jnp.concatenate([pair[0][f], pair[1][f]], axis=0).astype(jnp.bfloat16)
                for d in range(parts):
                    ready[w, d, f, pl.ds(m, 16), :] = both[:, d * tile_cols : (d + 1) * tile_cols]
        for kind in range(2):
            for p in range(parts - 1):
                part_copy(w, kind, p).start()
        own_copy(w).start()
        return carry

    lax.fori_loop(0, STEPS, wave, 0)

    for load in small:
        load.wait()

    def select(w, carry):
        ids = lax.broadcasted_iota(jnp.int32, (tile_cols, slots), 0) + wave_row(w) * tile_cols
        pick[pl.ds(pl.multiple_of(w * tile_cols, tile_cols), tile_cols), :] = jnp.where(
            ids == cells[...], 1.0, 0.0
        ).astype(jnp.bfloat16)
        return carry

    lax.fori_loop(0, waves, select, 0)
    chunk = 256 if slots % 256 == 0 else slots
    for s in range(0, slots, chunk):
        cut = slice(s, s + chunk)
        for i, third in enumerate(split(values[:, cut] + error[:, cut] * noise[cut, :].T)):
            target[i, :, cut] = third

    lax.fori_loop(STEPS, waves, wave, 0)

    def arrived(w):
        own_copy(w).wait()
        for p in range(parts - 1):
            part_copy(w, 0, p).wait_recv()

    def look(first, number, cut):
        seen = jnp.concatenate([recv[w, 0] for w in range(first, first + number)], axis=1)
        return mxu(seen, pick[first * tile_cols : (first + number) * tile_cols, cut])

    early = waves - 1
    for w in range(early):
        arrived(w)
    for s in range(0, slots, chunk):
        observed[:, s : s + chunk] = look(0, early, slice(s, s + chunk))
    arrived(early)
    slot_ids = lax.broadcasted_iota(jnp.int32, (1, slots), 1)
    weights = jnp.where(slot_ids < count[...], 1.0 / (error[...] * error[...]), 0.0)
    both = None
    for s in range(0, slots, chunk):
        cut = slice(s, s + chunk)
        yb = observed[:, cut] + look(early, 1, cut)
        spread = yb - jnp.sum(yb, axis=0, keepdims=True) * (1.0 / full)
        wh, wm, wl = split(spread * weights[:, cut])
        yb = yb.astype(jnp.bfloat16)
        dh, dm, dl = (target[i, :, cut] for i in range(3))

        def turned(a, b):
            return lax.dot_general(a, b, (((1,), (1,)), ((), ())), preferred_element_type=jnp.float32)

        one = turned(jnp.concatenate([yb, dh, dm], axis=0), jnp.concatenate([wh, wm], axis=0))
        two = turned(jnp.concatenate([yb, dh], axis=0), wl)
        three = turned(dl, wh)
        term = [one[:full, :full], one[:full, full:] + two[:full]]
        term += [one[full : 2 * full, :full]]
        term += [one[full : 2 * full, full:] + one[2 * full :, :full] + one[2 * full :, full:] + two[full:] + three]
        both = term if both is None else [a + b for a, b in zip(both, term)]
    plain = both[0] + both[1]
    aimed = both[2] + both[3]
    least = full - 1.0
    eye = jnp.where(
        lax.broadcasted_iota(jnp.int32, (full, full), 0) == lax.broadcasted_iota(jnp.int32, (full, full), 1), 1.0, 0.0
    )
    gram = plain - jnp.sum(plain, axis=0, keepdims=True) * (1.0 / full) + least * eye
    rhs = aimed - plain
    rhs = rhs - jnp.sum(rhs, axis=1, keepdims=True) * (1.0 / full)
    solved, eye = solve_turned(gram, rhs, least)
    mix = solved + eye
    upper = mix.astype(jnp.bfloat16)
    lower = (mix - upper.astype(jnp.float32)).astype(jnp.bfloat16)
    mix = jnp.concatenate([upper, lower], axis=1)
    for f in range(fields):
        for w in range(0, waves, 2):
            if f == 1:
                for i in (w, w + 1):
                    for p in range(parts - 1):
                        part_copy(i, 1, p).wait_recv()
            block = jnp.concatenate([recv[w, f], recv[w + 1, f]], axis=1)
            done = mxu(mix, jnp.concatenate([block, block], axis=0))
            for i in range(2):
                tall[f, pl.ds(wave_row(w + i), full, stride=rows), :] = done[:, i * tile_cols : (i + 1) * tile_cols]
        packed[f] = tall[f].reshape(full, rows, tile_cols).astype(jnp.bfloat16)
        pltpu.make_async_copy(packed.at[f], out_hbm.at[f], out_sem.at[f]).start()
    for way in range(2):
        for k in range(STEPS):
            halo_copy(way, k).wait_send()

    def finish(w, carry):
        for kind in range(2):
            for p in range(parts - 1):
                part_copy(w, kind, p).wait_send()
        return carry

    lax.fori_loop(0, waves, finish, 0)
    for f in range(fields):
        pltpu.make_async_copy(packed.at[f], out_hbm.at[f], out_sem.at[f]).wait()


def hbm():
    return pl.BlockSpec(memory_space=pltpu.HBM)


def body(members, obs_cells, obs_count, obs_values, obs_error, obs_noise):
    fields, ens, rows, cols = members.shape
    parts = lax.axis_size("mem")
    tile_cols = cols // parts
    full = ens * parts
    points = rows * tile_cols
    slots = obs_cells.shape[2]
    lines = rows + 2 * STEPS
    edge = pltpu.VMEM((2, STEPS, fields, ens, cols), jnp.bfloat16)
    row = pltpu.VMEM((1, slots), jnp.float32)
    dma = pltpu.SemaphoreType.DMA
    return pl.pallas_call(
        kernel,
        name="assimilate",
        out_shape=jax.ShapeDtypeStruct((fields, full, rows, tile_cols), jnp.bfloat16),
        in_specs=[hbm()] * 6,
        out_specs=hbm(),
        scratch_shapes=[
            pltpu.VMEM((STEPS * lines, fields, ens, cols), jnp.float32),
            edge,
            edge,
            pltpu.VMEM((rows, parts, fields, ens, tile_cols), jnp.bfloat16),
            pltpu.VMEM((rows, fields, full, tile_cols), jnp.bfloat16),
            pltpu.VMEM(obs_noise.shape[2:], jnp.float32),
            pltpu.VMEM((1, slots), jnp.int32),
            row,
            row,
            pltpu.VMEM((1, 1), jnp.int32),
            pltpu.VMEM((points, slots), jnp.bfloat16),
            pltpu.VMEM((3, full, slots), jnp.bfloat16),
            pltpu.VMEM((full, slots), jnp.float32),
            pltpu.VMEM((fields, full * rows, tile_cols), jnp.float32),
            pltpu.VMEM((fields, full, rows, tile_cols), jnp.bfloat16),
            dma((rows,)),
            dma((5,)),
            dma((2, STEPS)),
            dma((2, STEPS)),
            dma((rows, 2, parts - 1)),
            dma((rows, 2, parts - 1)),
            dma((rows,)),
            dma((fields,)),
        ],
        compiler_params=pltpu.CompilerParams(
            vmem_limit_bytes=VMEM_BYTES, collective_id=0, has_side_effects=True
        ),
    )(members, obs_count, obs_cells[0], obs_values[0], obs_error[0], obs_noise[0, 0])


def solution(mesh):
    in_specs = (
        P(None, "mem", ("tile", "grp"), None),
        P(("tile", "grp"), "mem", None),
        P(("tile", "grp"), "mem"),
        P(("tile", "grp"), "mem", None),
        P(("tile", "grp"), "mem", None),
        P(("tile", "grp"), "mem", None, None),
    )
    out_specs = P(None, None, ("tile", "grp"), "mem")
    return jax.shard_map(body, mesh=mesh, in_specs=in_specs, out_specs=out_specs, check_vma=False)
```

```python
import jax
import jax.numpy as jnp
from jax import lax
from jax.experimental import pallas as pl
from jax.experimental.pallas import tpu as pltpu
from jax.sharding import PartitionSpec as P

STEPS = 4
NEWTON_STEPS = 12

courant = 0.3
gravity = 1.0
coriolis = 0.1
VMEM_BYTES = 45000000
MESH = pl.DeviceIdType.MESH


def advance(west, mid, east):
    (hw, uw, vw), (h, u, v), (he, ue, ve) = west, mid, east
    cols = h.shape[1]
    north = lambda q: pltpu.roll(q, cols - 1, 1)
    south = lambda q: pltpu.roll(q, 1, 1)
    flux = courant * (v + h * v)
    near = 0.25 * h
    rise = ue - uw
    new_h = 0.25 * (he + hw) - courant * (rise + (he * ue - hw * uw)) + (north(near - flux) + south(near + flux))
    un, us = north(u), south(u)
    new_u = (
        (ue + uw) * (0.25 - (0.5 * courant) * rise)
        - (courant * gravity) * (he - hw)
        + (0.25 * (un + us) + v * (coriolis - courant * (un - us)))
    )
    flux = courant * (0.5 * (v * v) + gravity * h)
    near = 0.25 * v
    new_v = (
        0.25 * (ve + vw)
        - u * (coriolis + courant * (ve - vw))
        + (north(near - flux) + south(near + flux))
    )
    return new_h, new_u, new_v


def split(q):
    high = q.astype(jnp.bfloat16)
    rest = q - high.astype(jnp.float32)
    middle = rest.astype(jnp.bfloat16)
    return high, middle, (rest - middle.astype(jnp.float32)).astype(jnp.bfloat16)


def mxu(a, b):
    return jnp.dot(a, b, preferred_element_type=jnp.float32)


def product(a, b):
    (ah, am, al), (bh, bm, bl) = a, b
    size = bh.shape[1]
    top = mxu(
        jnp.concatenate([ah, am], axis=1),
        jnp.concatenate([jnp.concatenate([bh, bm], axis=1)] * 2, axis=0),
    )
    low = mxu(jnp.concatenate([ah, al], axis=1), jnp.concatenate([bl, bh], axis=0))
    return top[:, :size] + (top[:, size:] + low)


def solve_turned(gram, rhs, least):
    size = gram.shape[0]
    bound = jnp.max(jnp.sum(jnp.abs(gram), axis=0, keepdims=True), axis=1, keepdims=True)
    bound = jnp.broadcast_to(bound, (1, size))
    scale = 1.0 / bound
    eye = jnp.where(
        lax.broadcasted_iota(jnp.int32, (size, size), 0) == lax.broadcasted_iota(jnp.int32, (size, size), 1), 1.0, 0.0
    )
    low = least * scale
    y, x = gram * scale, eye * scale
    for _ in range(NEWTON_STEPS):
        mid = 1.0 + low
        gain = 4.0 / (mid * mid)
        low = gain * low
        parts = split(y)
        both = [jnp.concatenate(pair, axis=0) for pair in zip(parts, split(x))]
        done = product(both, parts)
        y = gain * (mid * y - done[:size])
        x = gain * (mid * x - done[size:])
    inverse = split(x)
    found = product(split(rhs), inverse)
    rest = rhs - product(split(found), split(gram))
    return found + product(split(rest), inverse), eye


def place_of(slab):
    groups = lax.axis_size("grp")
    return {"tile": slab // groups, "grp": lax.rem(slab, groups)}


def kernel(
    members_hbm, count_hbm, cells_hbm, values_hbm, error_hbm, noise_hbm, out,
    lev, edges, halo, ready, recv, noise, cells, values, error, count, pick, target, observed, tall,
    row_sem, load_sem, halo_send, halo_recv, part_send, part_recv, own_sem,
):
    fields, ens, rows, cols = members_hbm.shape
    waves = rows
    assert rows == 2 * STEPS
    lines = rows + 2 * STEPS
    parts, tile_cols = ready.shape[1], ready.shape[4]
    full = parts * ens
    slots = cells.shape[1]
    me = lax.axis_index("mem")
    total = lax.axis_size("tile") * lax.axis_size("grp")
    slab = lax.axis_index("tile") * lax.axis_size("grp") + lax.axis_index("grp")
    after, before = lax.rem(slab + 1, total), lax.rem(slab + total - 1, total)
    peers = [lax.rem(me + p, parts) for p in range(1, parts)]
    targets = [place_of(after), place_of(before)] + [{"mem": p} for p in peers]
    quick = 1 - lax.rem(lax.axis_index("grp"), 2)
    barrier = pltpu.get_barrier_semaphore()
    for target_id in targets:
        pl.semaphore_signal(barrier, inc=1, device_id=target_id, device_id_type=MESH)

    def row_load(r):
        return pltpu.make_async_copy(members_hbm.at[:, :, r, :], lev.at[STEPS + r], row_sem.at[r])

    small = [
        pltpu.make_async_copy(src, dst, load_sem.at[i])
        for i, (src, dst) in enumerate(
            ((noise_hbm, noise), (cells_hbm, cells), (values_hbm, values), (error_hbm, error), (count_hbm, count))
        )
    ]
    for k in range(STEPS):
        row_load(rows - 1 - k).start()
        row_load(k).start()
    for load in small:
        load.start()

    def halo_copy(way, k):
        return pltpu.make_async_remote_copy(
            src_ref=edges.at[way, k],
            dst_ref=halo.at[way, k],
            send_sem=halo_send.at[way, k],
            recv_sem=halo_recv.at[way, k],
            device_id=place_of(after + way * (before - after)),
            device_id_type=MESH,
        )

    patient = slab == (1 - quick) + quick * (total - 2)
    for k in range(STEPS):
        for way, r in ((0, rows - 1 - k), (1, k)):
            row_load(r).wait()
            edges[way, k] = lev[STEPS + r].astype(jnp.bfloat16)
        if k == 0:
            pl.semaphore_wait(barrier, len(targets))

        @pl.when(jnp.logical_not(patient))
        def _():
            halo_copy(quick, k).start()

        halo_copy(1 - quick, k).start()

    def stencil(base, half):
        def at(i):
            return [lev[i, f, pl.ds(half, 8), :] for f in range(fields)]

        return advance(at(base - 1), at(base), at(base + 1))

    def step_row(level, line):
        base = level * lines + line
        for m in range(0, ens, 8):
            done = stencil(base, m)
            for f in range(fields):
                lev[base + lines, f, pl.ds(m, 8), :] = done[f]

    for level in range(STEPS - 1):

        def inner_row(i, carry, level=level):
            step_row(level, STEPS + level + 1 + i)
            return carry

        lax.fori_loop(0, rows - 2 * (level + 1), inner_row, 0)

    @pl.when(patient)
    def _():
        for k in range(STEPS):
            halo_copy(quick, k).start()

    def wave_side(w):
        late = w // STEPS
        return quick + late - 2 * quick * late, lax.rem(w, STEPS)

    def wave_row(w):
        side, k = wave_side(w)
        return (STEPS - 1 - k) + side * (2 * k + 1)

    def part_copy(w, p):
        return pltpu.make_async_remote_copy(
            src_ref=ready.at[w, peers[p]],
            dst_ref=recv.at[w, :, pl.ds(me * ens, ens)],
            send_sem=part_send.at[w, p],
            recv_sem=part_recv.at[w, p],
            device_id={"mem": peers[p]},
            device_id_type=MESH,
        )

    def own_copy(w):
        return pltpu.make_async_copy(ready.at[w, me], recv.at[w, :, pl.ds(me * ens, ens)], own_sem.at[w])

    def wave(w, carry):
        side, k = wave_side(w)
        sign = 1 - 2 * side
        start = (STEPS - 1 - k) + side * (2 * k + lines - 2 * STEPS + 1)
        halo_copy(side, k).wait_recv()
        lev[start] = halo[side, k].astype(jnp.float32)

        def up(level, c):
            step_row(level, start + sign * (level + 1))
            return c

        lax.fori_loop(0, STEPS - 1, up, 0)
        base = (STEPS - 1) * lines + start + sign * STEPS
        for m in range(0, ens, 16):
            pair = [stencil(base, m), stencil(base, m + 8)]
            for f in range(fields):
                both = jnp.concatenate([pair[0][f], pair[1][f]], axis=0).astype(jnp.bfloat16)
                for d in range(parts):
                    ready[w, d, f, pl.ds(m, 16), :] = both[:, d * tile_cols : (d + 1) * tile_cols]
        for p in range(parts - 1):
            part_copy(w, p).start()
        own_copy(w).start()
        return carry

    lax.fori_loop(0, STEPS, wave, 0)

    for load in small:
        load.wait()

    def select(w, carry):
        ids = lax.broadcasted_iota(jnp.int32, (tile_cols, slots), 0) + wave_row(w) * tile_cols
        pick[pl.ds(pl.multiple_of(w * tile_cols, tile_cols), tile_cols), :] = jnp.where(
            ids == cells[...], 1.0, 0.0
        ).astype(jnp.bfloat16)
        return carry

    lax.fori_loop(0, waves, select, 0)
    chunk = 256 if slots % 256 == 0 else slots
    for s in range(0, slots, chunk):
        cut = slice(s, s + chunk)
        for i, third in enumerate(split(values[:, cut] + error[:, cut] * noise[cut, :].T)[:2]):
            target[i, :, cut] = third

    lax.fori_loop(STEPS, waves, wave, 0)

    def arrived(w):
        own_copy(w).wait()
        for p in range(parts - 1):
            part_copy(w, p).wait_recv()

    def look(first, number, cut):
        seen = jnp.concatenate([recv[w, 0] for w in range(first, first + number)], axis=1)
        return mxu(seen, pick[first * tile_cols : (first + number) * tile_cols, cut])

    early = waves - 1
    for w in range(early):
        arrived(w)
    for s in range(0, slots, chunk):
        observed[:, s : s + chunk] = look(0, early, slice(s, s + chunk))
    arrived(early)
    slot_ids = lax.broadcasted_iota(jnp.int32, (1, slots), 1)
    weights = jnp.where(slot_ids < count[...], 1.0 / (error[...] * error[...]), 0.0)
    both = None
    for s in range(0, slots, chunk):
        cut = slice(s, s + chunk)
        yb = observed[:, cut] + look(early, 1, cut)
        spread = yb - jnp.sum(yb, axis=0, keepdims=True) * (1.0 / full)
        wh, wm, wl = split(spread * weights[:, cut])
        yb = yb.astype(jnp.bfloat16)
        dh, dm = (target[i, :, cut] for i in range(2))

        def turned(a, b):
            return lax.dot_general(a, b, (((1,), (1,)), ((), ())), preferred_element_type=jnp.float32)

        one = turned(jnp.concatenate([yb, dh, dm], axis=0), jnp.concatenate([wh, wm], axis=0))
        two = turned(yb, wl)
        term = [one[:full, :full], one[:full, full:] + two]
        term += [one[full : 2 * full, :full]]
        term += [one[full : 2 * full, full:] + one[2 * full :, :full] + one[2 * full :, full:]]
        both = term if both is None else [a + b for a, b in zip(both, term)]
    plain = both[0] + both[1]
    aimed = both[2] + both[3]
    least = full - 1.0
    eye = jnp.where(
        lax.broadcasted_iota(jnp.int32, (full, full), 0) == lax.broadcasted_iota(jnp.int32, (full, full), 1), 1.0, 0.0
    )
    gram = plain - jnp.sum(plain, axis=0, keepdims=True) * (1.0 / full) + least * eye
    rhs = aimed - plain
    rhs = rhs - jnp.sum(rhs, axis=1, keepdims=True) * (1.0 / full)
    solved, eye = solve_turned(gram, rhs, least)
    mix = solved + eye
    upper = mix.astype(jnp.bfloat16)
    lower = (mix - upper.astype(jnp.float32)).astype(jnp.bfloat16)
    mix = jnp.concatenate([upper, lower], axis=1)
    for f in range(fields):
        for w in range(0, waves, 2):
            block = jnp.concatenate([recv[w, f], recv[w + 1, f]], axis=1)
            done = mxu(mix, jnp.concatenate([block, block], axis=0))
            for i in range(2):
                tall[f, pl.ds(wave_row(w + i), full, stride=rows), :] = done[:, i * tile_cols : (i + 1) * tile_cols]
        out[f] = tall[f].reshape(full, rows, tile_cols).astype(jnp.bfloat16)
    for way in range(2):
        for k in range(STEPS):
            halo_copy(way, k).wait_send()

    def finish(w, carry):
        for p in range(parts - 1):
            part_copy(w, p).wait_send()
        return carry

    lax.fori_loop(0, waves, finish, 0)


def hbm():
    return pl.BlockSpec(memory_space=pltpu.HBM)


def stay(q):
    return pltpu.with_memory_space_constraint(q, pltpu.HBM)


def body(members, obs_cells, obs_count, obs_values, obs_error, obs_noise):
    fields, ens, rows, cols = members.shape
    parts = lax.axis_size("mem")
    tile_cols = cols // parts
    full = ens * parts
    points = rows * tile_cols
    slots = obs_cells.shape[2]
    lines = rows + 2 * STEPS
    edge = pltpu.VMEM((2, STEPS, fields, ens, cols), jnp.bfloat16)
    row = pltpu.VMEM((1, slots), jnp.float32)
    dma = pltpu.SemaphoreType.DMA
    return pl.pallas_call(
        kernel,
        name="assimilate",
        out_shape=jax.ShapeDtypeStruct((fields, full, rows, tile_cols), jnp.bfloat16),
        in_specs=[hbm()] * 6,
        out_specs=pl.BlockSpec(memory_space=pltpu.VMEM),
        scratch_shapes=[
            pltpu.VMEM((STEPS * lines, fields, ens, cols), jnp.float32),
            edge,
            edge,
            pltpu.VMEM((rows, parts, fields, ens, tile_cols), jnp.bfloat16),
            pltpu.VMEM((rows, fields, full, tile_cols), jnp.bfloat16),
            pltpu.VMEM(obs_noise.shape[2:], jnp.float32),
            pltpu.VMEM((1, slots), jnp.int32),
            row,
            row,
            pltpu.VMEM((1, 1), jnp.int32),
            pltpu.VMEM((points, slots), jnp.bfloat16),
            pltpu.VMEM((2, full, slots), jnp.bfloat16),
            pltpu.VMEM((full, slots), jnp.float32),
            pltpu.VMEM((fields, full * rows, tile_cols), jnp.float32),
            dma((rows,)),
            dma((5,)),
            dma((2, STEPS)),
            dma((2, STEPS)),
            dma((rows, parts - 1)),
            dma((rows, parts - 1)),
            dma((rows,)),
        ],
        compiler_params=pltpu.CompilerParams(
            vmem_limit_bytes=VMEM_BYTES, collective_id=0, has_side_effects=True
        ),
    )(stay(members), obs_count, *[stay(q) for q in (obs_cells[0], obs_values[0], obs_error[0], obs_noise[0, 0])])


def solution(mesh):
    in_specs = (
        P(None, "mem", ("tile", "grp"), None),
        P(("tile", "grp"), "mem", None),
        P(("tile", "grp"), "mem"),
        P(("tile", "grp"), "mem", None),
        P(("tile", "grp"), "mem", None),
        P(("tile", "grp"), "mem", None, None),
    )
    out_specs = P(None, None, ("tile", "grp"), "mem")
    return jax.shard_map(body, mesh=mesh, in_specs=in_specs, out_specs=out_specs, check_vma=False)
```

```python
import jax
import jax.numpy as jnp
from jax import lax
from jax.experimental import pallas as pl
from jax.experimental.pallas import tpu as pltpu
from jax.sharding import PartitionSpec as P

STEPS = 4
NEWTON_STEPS = 12
LAST = 2

courant = 0.3
gravity = 1.0
coriolis = 0.1
VMEM_BYTES = 45000000
MESH = pl.DeviceIdType.MESH


def advance(west, mid, east):
    (hw, uw, vw), (h, u, v), (he, ue, ve) = west, mid, east
    cols = h.shape[1]
    north = lambda q: pltpu.roll(q, cols - 1, 1)
    south = lambda q: pltpu.roll(q, 1, 1)
    flux = courant * (v + h * v)
    near = 0.25 * h
    rise = ue - uw
    new_h = 0.25 * (he + hw) - courant * (rise + (he * ue - hw * uw)) + (north(near - flux) + south(near + flux))
    un, us = north(u), south(u)
    new_u = (
        (ue + uw) * (0.25 - (0.5 * courant) * rise)
        - (courant * gravity) * (he - hw)
        + (0.25 * (un + us) + v * (coriolis - courant * (un - us)))
    )
    flux = courant * (0.5 * (v * v) + gravity * h)
    near = 0.25 * v
    new_v = (
        0.25 * (ve + vw)
        - u * (coriolis + courant * (ve - vw))
        + (north(near - flux) + south(near + flux))
    )
    return new_h, new_u, new_v


def known(mid, far, toward):
    (h, u, v), (hf, uf, vf) = mid, far
    cols = h.shape[1]
    north = lambda q: pltpu.roll(q, cols - 1, 1)
    south = lambda q: pltpu.roll(q, 1, 1)
    flux = courant * (v + h * v)
    near = 0.25 * h
    new_h = 0.25 * hf - toward * (uf + hf * uf) + (north(near - flux) + south(near + flux))
    un, us = north(u), south(u)
    new_u = uf * (0.25 - (0.5 * toward) * uf) - (toward * gravity) * hf
    new_u = new_u + (0.25 * (un + us) + v * (coriolis - courant * (un - us)))
    flux = courant * (0.5 * (v * v) + gravity * h)
    near = 0.25 * v
    turn = toward * u
    new_v = vf * (0.25 - turn) - coriolis * u + (north(near - flux) + south(near + flux))
    return new_h, new_u, new_v, 0.25 + turn


def joined(row, rest, toward):
    (h, u, v), (rest_h, rest_u, rest_v, turn) = row, rest
    return (
        rest_h + (0.25 * h + toward * (u + h * u)),
        rest_u + (u * (0.25 + (0.5 * toward) * u) + (toward * gravity) * h),
        rest_v + v * turn,
    )


def split(q):
    high = q.astype(jnp.bfloat16)
    rest = q - high.astype(jnp.float32)
    middle = rest.astype(jnp.bfloat16)
    return high, middle, (rest - middle.astype(jnp.float32)).astype(jnp.bfloat16)


def mxu(a, b):
    return jnp.dot(a, b, preferred_element_type=jnp.float32)


def product(a, b):
    (ah, am, al), (bh, bm, bl) = a, b
    size = bh.shape[1]
    top = mxu(
        jnp.concatenate([ah, am], axis=1),
        jnp.concatenate([jnp.concatenate([bh, bm], axis=1)] * 2, axis=0),
    )
    low = mxu(jnp.concatenate([ah, al], axis=1), jnp.concatenate([bl, bh], axis=0))
    return top[:, :size] + (top[:, size:] + low)


def solve_turned(gram, rhs, least):
    size = gram.shape[0]
    bound = jnp.max(jnp.sum(jnp.abs(gram), axis=0, keepdims=True), axis=1, keepdims=True)
    bound = jnp.broadcast_to(bound, (1, size))
    scale = 1.0 / bound
    eye = jnp.where(
        lax.broadcasted_iota(jnp.int32, (size, size), 0) == lax.broadcasted_iota(jnp.int32, (size, size), 1), 1.0, 0.0
    )
    low = least * scale
    y, x = gram * scale, eye * scale
    for _ in range(NEWTON_STEPS):
        mid = 1.0 + low
        gain = 4.0 / (mid * mid)
        low = gain * low
        parts = split(y)
        both = [jnp.concatenate(pair, axis=0) for pair in zip(parts, split(x))]
        done = product(both, parts)
        y = gain * (mid * y - done[:size])
        x = gain * (mid * x - done[size:])
    inverse = split(x)
    found = product(split(rhs), inverse)
    rest = rhs - product(split(found), split(gram))
    return found + product(split(rest), inverse), eye


def place_of(slab):
    groups = lax.axis_size("grp")
    return {"tile": slab // groups, "grp": lax.rem(slab, groups)}


def kernel(
    members_hbm, count_hbm, cells_hbm, values_hbm, error_hbm, noise_hbm, out,
    lev, edges, halo, ready, recv, partial, noise, cells, values, error, count, pick, target, wanted, heavy, tall,
    row_sem, load_sem, halo_send, halo_recv, part_send, part_recv, own_sem,
):
    fields, ens, rows, cols = members_hbm.shape
    waves = rows
    assert rows == 2 * STEPS
    lines = rows + 2 * STEPS
    parts, tile_cols = ready.shape[1], ready.shape[4]
    full = parts * ens
    slots = cells.shape[1]
    points = rows * tile_cols
    me = lax.axis_index("mem")
    total = lax.axis_size("tile") * lax.axis_size("grp")
    slab = lax.axis_index("tile") * lax.axis_size("grp") + lax.axis_index("grp")
    after, before = lax.rem(slab + 1, total), lax.rem(slab + total - 1, total)
    peers = [lax.rem(me + p, parts) for p in range(1, parts)]
    targets = [place_of(after), place_of(before)] + [{"mem": p} for p in peers]
    quick = 1 - lax.rem(lax.axis_index("grp"), 2)
    barrier = pltpu.get_barrier_semaphore()
    for target_id in targets:
        pl.semaphore_signal(barrier, inc=1, device_id=target_id, device_id_type=MESH)

    def row_load(r):
        return pltpu.make_async_copy(members_hbm.at[:, :, r, :], lev.at[STEPS + r], row_sem.at[r])

    small = [
        pltpu.make_async_copy(src, dst, load_sem.at[i])
        for i, (src, dst) in enumerate(
            ((noise_hbm, noise), (cells_hbm, cells), (values_hbm, values), (error_hbm, error), (count_hbm, count))
        )
    ]
    for k in range(STEPS):
        row_load(rows - 1 - k).start()
        row_load(k).start()
    for load in small:
        load.start()

    def halo_copy(way, k):
        return pltpu.make_async_remote_copy(
            src_ref=edges.at[way, k],
            dst_ref=halo.at[way, k],
            send_sem=halo_send.at[way, k],
            recv_sem=halo_recv.at[way, k],
            device_id=place_of(after + way * (before - after)),
            device_id_type=MESH,
        )

    patient = slab == (1 - quick) + quick * (total - 2)
    for k in range(STEPS):
        for way, r in ((0, rows - 1 - k), (1, k)):
            row_load(r).wait()
            edges[way, k] = lev[STEPS + r].astype(jnp.bfloat16)
        if k == 0:
            pl.semaphore_wait(barrier, len(targets))

        @pl.when(jnp.logical_not(patient))
        def _():
            halo_copy(quick, k).start()

        halo_copy(1 - quick, k).start()

    def stencil(base, half):
        def at(i):
            return [lev[i, f, pl.ds(half, 8), :] for f in range(fields)]

        return advance(at(base - 1), at(base), at(base + 1))

    def step_row(level, line):
        base = level * lines + line
        for m in range(0, ens, 8):
            done = stencil(base, m)
            for f in range(fields):
                lev[base + lines, f, pl.ds(m, 8), :] = done[f]

    for level in range(STEPS - 1):

        def inner_row(i, carry, level=level):
            step_row(level, STEPS + level + 1 + i)
            return carry

        lax.fori_loop(0, rows - 2 * (level + 1), inner_row, 0)
        if level == 0:
            @pl.when(patient)
            def _():
                for k in range(STEPS):
                    halo_copy(quick, k).start()


    def wave_side(w):
        late = w // STEPS
        return quick + late - 2 * quick * late, lax.rem(w, STEPS)

    def wave_row(w):
        side, k = wave_side(w)
        return (STEPS - 1 - k) + side * (2 * k + 1)

    def part_copy(w, p, kind=0):
        here = ((0, fields), (0, 1), (1, fields - 1))[kind]
        slot = w + kind // 2 * LAST
        return pltpu.make_async_remote_copy(
            src_ref=ready.at[w, peers[p], pl.ds(*here)],
            dst_ref=recv.at[w, pl.ds(*here), pl.ds(me * ens, ens)],
            send_sem=part_send.at[slot, p],
            recv_sem=part_recv.at[slot, p],
            device_id={"mem": peers[p]},
            device_id_type=MESH,
        )

    def own_copy(w):
        return pltpu.make_async_copy(ready.at[w, me], recv.at[w, :, pl.ds(me * ens, ens)], own_sem.at[w])

    def place(w):
        side, k = wave_side(w)
        return side, k, 1 - 2 * side, (STEPS - 1 - k) + side * (2 * k + lines - 2 * STEPS + 1)

    def make_ready(w, m, pair):
        for f in range(fields):
            both = jnp.concatenate([pair[0][f], pair[1][f]], axis=0).astype(jnp.bfloat16)
            for d in range(parts):
                ready[w, d, f, pl.ds(m, 16), :] = both[:, d * tile_cols : (d + 1) * tile_cols]

    def wave(w, carry):
        side, k, sign, start = place(w)
        halo_copy(side, k).wait_recv()
        lev[start] = halo[side, k].astype(jnp.float32)

        def up(level, c):
            step_row(level, start + sign * (level + 1))
            return c

        lax.fori_loop(0, STEPS - 1, up, 0)
        base = (STEPS - 1) * lines + start + sign * STEPS
        for m in range(0, ens, 16):
            make_ready(w, m, [stencil(base, m), stencil(base, m + 8)])
        for p in range(parts - 1):
            part_copy(w, p).start()
        own_copy(w).start()
        return carry

    def late_wave(w, kind, last=False):
        side, k, sign, start = place(w)
        toward = courant * sign.astype(jnp.float32)

        def prepare(level, c):
            base = level * lines + start + sign * (level + 1)
            for m in range(0, ens, 8):
                mid, far = ([lev[i, f, pl.ds(m, 8), :] for f in range(fields)] for i in (base, base + sign))
                for i, q in enumerate(known(mid, far, toward)):
                    partial[level, i, pl.ds(m, 8), :] = q
            return c

        lax.fori_loop(0, STEPS, prepare, 0)
        halo_copy(side, k).wait_recv()
        for m in range(0, ens, 16):
            rows16 = [halo[side, k, f, pl.ds(m, 16), :].astype(jnp.float32) for f in range(fields)]
            pair = []
            for half in range(2):
                now = [q[8 * half : 8 * half + 8] for q in rows16]
                here = pl.ds(m + 8 * half, 8)
                for level in range(STEPS):
                    if not last:
                        for f in range(fields):
                            lev[level * lines + start + sign * level, f, here, :] = now[f]
                    now = joined(now, [partial[level, i, here, :] for i in range(fields + 1)], toward)
                pair.append(now)
            make_ready(w, m, pair)
        for p in range(parts - 1):
            part_copy(w, p, kind).start()
        own_copy(w).start()

    def late_loop(w, carry):
        late_wave(w, 0)
        return carry

    lax.fori_loop(0, STEPS, wave, 0)

    lax.fori_loop(STEPS, waves - LAST, late_loop, 0)
    for w in range(waves - LAST, waves):
        late_wave(w, 1, w == waves - 1)
    for w in range(waves - LAST, waves):
        for p in range(parts - 1):
            part_copy(w, p, 2).start()

    def arrived(w):
        own_copy(w).wait()
        for p in range(parts - 1):
            part_copy(w, p, 1 if w >= waves - LAST else 0).wait_recv()

    for load in small:
        load.wait()

    def select(w, carry):
        ids = lax.broadcasted_iota(jnp.int32, (tile_cols, slots), 0) + wave_row(w) * tile_cols
        pick[pl.ds(pl.multiple_of(w * tile_cols, tile_cols), tile_cols), :] = jnp.where(
            ids == cells[...], 1.0, 0.0
        ).astype(jnp.bfloat16)
        return carry

    lax.fori_loop(0, waves, select, 0)
    slot_ids = lax.broadcasted_iota(jnp.int32, (1, slots), 1)
    weights = jnp.where(slot_ids < count[...], 1.0 / (error[...] * error[...]), 0.0)
    chunk = 256 if slots % 256 == 0 else slots
    for s in range(0, slots, chunk):
        cut = slice(s, s + chunk)
        asked = weights[:, cut] * (values[:, cut] + error[:, cut] * noise[cut, :].T)
        for i, third in enumerate(split(asked)[:2]):
            target[i * full : (i + 1) * full, cut] = third
    line_ids = lax.broadcasted_iota(jnp.int32, (16, slots), 0)
    thirds = [q.astype(jnp.float32) for q in split(weights)]
    target[2 * full :, :] = jnp.where(
        line_ids == 0, thirds[0], jnp.where(line_ids == 1, thirds[1], jnp.where(line_ids == 2, thirds[2], 0.0))
    ).astype(jnp.bfloat16)

    def turned(a, b):
        return lax.dot_general(a, b, (((1,), (1,)), ((), ())), preferred_element_type=jnp.float32)

    chunk = 2 * tile_cols
    for c in range(0, points, chunk):
        cut = slice(c, c + chunk)
        summed = turned(target[...], pick[cut, :])
        for i, third in enumerate(split(summed[:full] + summed[full : 2 * full])[:2]):
            wanted[i * full : (i + 1) * full, cut] = third
        tail = summed[2 * full :]
        heavy[:, cut] = tail[0:1] + (tail[1:2] + tail[2:3])

    def observe(first, number):
        cut = slice(first * tile_cols, (first + number) * tile_cols)
        seen = jnp.concatenate([recv[w, 0] for w in range(first, first + number)], axis=1)
        near = seen.astype(jnp.float32)
        spread = near - jnp.sum(near, axis=0, keepdims=True) * (1.0 / full)
        wh, wm, wl = split(spread * heavy[:, cut])
        one = turned(seen, jnp.concatenate([wh, wm], axis=0))
        plain = one[:, :full] + (one[:, full:] + turned(seen, wl))
        two = turned(wanted[:, cut], seen)
        return plain, two[:full] + two[full:]

    early = waves - 1
    for w in range(early):
        arrived(w)
    plain, aimed = observe(0, early)
    arrived(early)
    plain, aimed = (a + b for a, b in zip((plain, aimed), observe(early, 1)))
    least = full - 1.0
    eye = jnp.where(
        lax.broadcasted_iota(jnp.int32, (full, full), 0) == lax.broadcasted_iota(jnp.int32, (full, full), 1), 1.0, 0.0
    )
    gram = plain - jnp.sum(plain, axis=0, keepdims=True) * (1.0 / full) + least * eye
    rhs = aimed - plain
    rhs = rhs - jnp.sum(rhs, axis=1, keepdims=True) * (1.0 / full)
    solved, eye = solve_turned(gram, rhs, least)
    mix = solved + eye
    upper = mix.astype(jnp.bfloat16)
    lower = (mix - upper.astype(jnp.float32)).astype(jnp.bfloat16)
    mix = jnp.concatenate([upper, lower], axis=1)
    for f in range(fields):
        for w in range(0, waves, 2):
            if f == 1:
                for i in (w, w + 1):
                    if i >= waves - LAST:
                        for p in range(parts - 1):
                            part_copy(i, p, 2).wait_recv()
            block = jnp.concatenate([recv[w, f], recv[w + 1, f]], axis=1)
            done = mxu(mix, jnp.concatenate([block, block], axis=0))
            for i in range(2):
                tall[f, pl.ds(wave_row(w + i), full, stride=rows), :] = done[:, i * tile_cols : (i + 1) * tile_cols]
        out[f] = tall[f].reshape(full, rows, tile_cols).astype(jnp.bfloat16)
    for way in range(2):
        for k in range(STEPS):
            halo_copy(way, k).wait_send()

    def finish(w, carry):
        for p in range(parts - 1):
            part_copy(w, p).wait_send()
        return carry

    lax.fori_loop(0, waves - LAST, finish, 0)
    for w in range(waves - LAST, waves):
        for kind in (1, 2):
            for p in range(parts - 1):
                part_copy(w, p, kind).wait_send()


def hbm():
    return pl.BlockSpec(memory_space=pltpu.HBM)


def stay(q):
    return pltpu.with_memory_space_constraint(q, pltpu.HBM)


def body(members, obs_cells, obs_count, obs_values, obs_error, obs_noise):
    fields, ens, rows, cols = members.shape
    parts = lax.axis_size("mem")
    tile_cols = cols // parts
    full = ens * parts
    points = rows * tile_cols
    slots = obs_cells.shape[2]
    lines = rows + 2 * STEPS
    edge = pltpu.VMEM((2, STEPS, fields, ens, cols), jnp.bfloat16)
    row = pltpu.VMEM((1, slots), jnp.float32)
    dma = pltpu.SemaphoreType.DMA
    return pl.pallas_call(
        kernel,
        name="assimilate",
        out_shape=jax.ShapeDtypeStruct((fields, full, rows, tile_cols), jnp.bfloat16),
        in_specs=[hbm()] * 6,
        out_specs=pl.BlockSpec(memory_space=pltpu.VMEM),
        scratch_shapes=[
            pltpu.VMEM((STEPS * lines, fields, ens, cols), jnp.float32),
            edge,
            edge,
            pltpu.VMEM((rows, parts, fields, ens, tile_cols), jnp.bfloat16),
            pltpu.VMEM((rows, fields, full, tile_cols), jnp.bfloat16),
            pltpu.VMEM((STEPS, fields + 1, ens, cols), jnp.float32),
            pltpu.VMEM(obs_noise.shape[2:], jnp.float32),
            pltpu.VMEM((1, slots), jnp.int32),
            row,
            row,
            pltpu.VMEM((1, 1), jnp.int32),
            pltpu.VMEM((points, slots), jnp.bfloat16),
            pltpu.VMEM((2 * full + 16, slots), jnp.bfloat16),
            pltpu.VMEM((2 * full, points), jnp.bfloat16),
            pltpu.VMEM((1, points), jnp.float32),
            pltpu.VMEM((fields, full * rows, tile_cols), jnp.float32),
            dma((rows,)),
            dma((5,)),
            dma((2, STEPS)),
            dma((2, STEPS)),
            dma((rows + LAST, parts - 1)),
            dma((rows + LAST, parts - 1)),
            dma((rows,)),
        ],
        compiler_params=pltpu.CompilerParams(
            vmem_limit_bytes=VMEM_BYTES, collective_id=0, has_side_effects=True
        ),
    )(stay(members), obs_count, *[stay(q) for q in (obs_cells[0], obs_values[0], obs_error[0], obs_noise[0, 0])])


def solution(mesh):
    in_specs = (
        P(None, "mem", ("tile", "grp"), None),
        P(("tile", "grp"), "mem", None),
        P(("tile", "grp"), "mem"),
        P(("tile", "grp"), "mem", None),
        P(("tile", "grp"), "mem", None),
        P(("tile", "grp"), "mem", None, None),
    )
    out_specs = P(None, None, ("tile", "grp"), "mem")
    return jax.shard_map(body, mesh=mesh, in_specs=in_specs, out_specs=out_specs, check_vma=False)
```

```python
import jax
import jax.numpy as jnp
from jax import lax
from jax.experimental import pallas as pl
from jax.experimental.pallas import tpu as pltpu
from jax.sharding import PartitionSpec as P

STEPS = 4
NEWTON_STEPS = 11
LAST = 2

courant = 0.3
gravity = 1.0
coriolis = 0.1
VMEM_BYTES = 45000000
MESH = pl.DeviceIdType.MESH


def advance(west, mid, east):
    (hw, uw, vw), (h, u, v), (he, ue, ve) = west, mid, east
    cols = h.shape[1]
    north = lambda q: pltpu.roll(q, cols - 1, 1)
    south = lambda q: pltpu.roll(q, 1, 1)
    flux = courant * (v + h * v)
    near = 0.25 * h
    rise = ue - uw
    new_h = 0.25 * (he + hw) - courant * (rise + (he * ue - hw * uw)) + (north(near - flux) + south(near + flux))
    un, us = north(u), south(u)
    new_u = (
        (ue + uw) * (0.25 - (0.5 * courant) * rise)
        - (courant * gravity) * (he - hw)
        + (0.25 * (un + us) + v * (coriolis - courant * (un - us)))
    )
    flux = courant * (0.5 * (v * v) + gravity * h)
    near = 0.25 * v
    new_v = (
        0.25 * (ve + vw)
        - u * (coriolis + courant * (ve - vw))
        + (north(near - flux) + south(near + flux))
    )
    return new_h, new_u, new_v


def known(mid, far, toward):
    (h, u, v), (hf, uf, vf) = mid, far
    cols = h.shape[1]
    north = lambda q: pltpu.roll(q, cols - 1, 1)
    south = lambda q: pltpu.roll(q, 1, 1)
    flux = courant * (v + h * v)
    near = 0.25 * h
    new_h = 0.25 * hf - toward * (uf + hf * uf) + (north(near - flux) + south(near + flux))
    un, us = north(u), south(u)
    new_u = uf * (0.25 - (0.5 * toward) * uf) - (toward * gravity) * hf
    new_u = new_u + (0.25 * (un + us) + v * (coriolis - courant * (un - us)))
    flux = courant * (0.5 * (v * v) + gravity * h)
    near = 0.25 * v
    turn = toward * u
    new_v = vf * (0.25 - turn) - coriolis * u + (north(near - flux) + south(near + flux))
    return new_h, new_u, new_v, 0.25 + turn


def joined(row, rest, toward):
    (h, u, v), (rest_h, rest_u, rest_v, turn) = row, rest
    return (
        rest_h + (0.25 * h + toward * (u + h * u)),
        rest_u + (u * (0.25 + (0.5 * toward) * u) + (toward * gravity) * h),
        rest_v + v * turn,
    )


def split(q):
    high = q.astype(jnp.bfloat16)
    rest = q - high.astype(jnp.float32)
    middle = rest.astype(jnp.bfloat16)
    return high, middle, (rest - middle.astype(jnp.float32)).astype(jnp.bfloat16)


def mxu(a, b):
    return jnp.dot(a, b, preferred_element_type=jnp.float32)


def product(a, b, fine=True):
    (ah, am, al), (bh, bm, bl) = a, b
    size = bh.shape[1]
    top = mxu(
        jnp.concatenate([ah, am], axis=1),
        jnp.concatenate([jnp.concatenate([bh, bm], axis=1)] * 2, axis=0),
    )
    if not fine:
        return top[:, :size] + top[:, size:]
    low = mxu(jnp.concatenate([ah, al], axis=1), jnp.concatenate([bl, bh], axis=0))
    return top[:, :size] + (top[:, size:] + low)


def solve_turned(gram, rhs, least):
    size = gram.shape[0]
    bound = jnp.max(jnp.sum(jnp.abs(gram), axis=0, keepdims=True), axis=1, keepdims=True)
    bound = jnp.broadcast_to(bound, (1, size))
    scale = 1.0 / bound
    eye = jnp.where(
        lax.broadcasted_iota(jnp.int32, (size, size), 0) == lax.broadcasted_iota(jnp.int32, (size, size), 1), 1.0, 0.0
    )
    low = least * scale
    y, x = gram * scale, eye * scale
    for step in range(NEWTON_STEPS):
        mid = 1.0 + low
        gain = 4.0 / (mid * mid)
        low = gain * low
        parts = split(y)
        both = [jnp.concatenate(pair, axis=0) for pair in zip(parts, split(x))]
        done = product(both, parts, step < NEWTON_STEPS - 4)
        y = gain * (mid * y - done[:size])
        x = gain * (mid * x - done[size:])
    inverse = split(x)
    found = product(split(rhs), inverse, False)
    rest = rhs - product(split(found), split(gram))
    return found + product(split(rest), inverse, False), eye


def place_of(slab):
    groups = lax.axis_size("grp")
    return {"tile": slab // groups, "grp": lax.rem(slab, groups)}


def kernel(
    members_hbm, count_hbm, cells_hbm, values_hbm, error_hbm, noise_hbm, out,
    lev, edges, halo, ready, recv, partial, noise, cells, values, error, count, pick, target, wanted, heavy, tall,
    row_sem, load_sem, halo_send, halo_recv, part_send, part_recv,
):
    fields, ens, rows, cols = members_hbm.shape
    waves = rows
    assert rows == 2 * STEPS
    lines = rows + 2 * STEPS
    parts, tile_cols = ready.shape[1], ready.shape[4]
    full = parts * ens
    slots = cells.shape[1]
    points = rows * tile_cols
    me = lax.axis_index("mem")
    total = lax.axis_size("tile") * lax.axis_size("grp")
    slab = lax.axis_index("tile") * lax.axis_size("grp") + lax.axis_index("grp")
    after, before = lax.rem(slab + 1, total), lax.rem(slab + total - 1, total)
    peers = [lax.rem(me + p, parts) for p in range(1, parts)]
    targets = [place_of(after), place_of(before)] + [{"mem": p} for p in peers]
    quick = 1 - lax.rem(lax.axis_index("grp"), 2)
    barrier = pltpu.get_barrier_semaphore()
    for target_id in targets:
        pl.semaphore_signal(barrier, inc=1, device_id=target_id, device_id_type=MESH)

    def row_load(r):
        return pltpu.make_async_copy(members_hbm.at[:, :, r, :], lev.at[STEPS + r], row_sem.at[r])

    small = [
        pltpu.make_async_copy(src, dst, load_sem.at[i])
        for i, (src, dst) in enumerate(
            ((noise_hbm, noise), (cells_hbm, cells), (values_hbm, values), (error_hbm, error), (count_hbm, count))
        )
    ]
    for k in range(STEPS):
        row_load(rows - 1 - k).start()
        row_load(k).start()
    for load in small:
        load.start()

    def halo_copy(way, k):
        return pltpu.make_async_remote_copy(
            src_ref=edges.at[way, k],
            dst_ref=halo.at[way, k],
            send_sem=halo_send,
            recv_sem=halo_recv.at[way, k],
            device_id=place_of(after + way * (before - after)),
            device_id_type=MESH,
        )

    patient = slab == (1 - quick) + quick * (total - 2)
    for k in range(STEPS):
        for way, r in ((0, rows - 1 - k), (1, k)):
            row_load(r).wait()
            edges[way, k] = lev[STEPS + r].astype(jnp.bfloat16)
        if k == 0:
            pl.semaphore_wait(barrier, len(targets))

        @pl.when(jnp.logical_not(patient))
        def _():
            halo_copy(quick, k).start()

        halo_copy(1 - quick, k).start()

    def stencil(base, half):
        def at(i):
            return [lev[i, f, pl.ds(half, 8), :] for f in range(fields)]

        return advance(at(base - 1), at(base), at(base + 1))

    def step_row(level, line):
        base = level * lines + line
        for m in range(0, ens, 8):
            done = stencil(base, m)
            for f in range(fields):
                lev[base + lines, f, pl.ds(m, 8), :] = done[f]

    for level in range(STEPS - 1):

        def inner_row(i, carry, level=level):
            step_row(level, STEPS + level + 1 + i)
            return carry

        lax.fori_loop(0, rows - 2 * (level + 1), inner_row, 0)
        if level == 0:
            @pl.when(patient)
            def _():
                for k in range(STEPS):
                    halo_copy(quick, k).start()


    def wave_side(w):
        late = w // STEPS
        return quick + late - 2 * quick * late, lax.rem(w, STEPS)

    def wave_row(w):
        side, k = wave_side(w)
        return (STEPS - 1 - k) + side * (2 * k + 1)

    def span(w, kind):
        return pl.ds(*((0, fields), (0, 1), (1, fields - 1))[kind]), part_recv.at[w + kind // 2 * LAST]

    def part_start(w, kind):
        here, landed = span(w, kind)
        for peer in peers:
            pltpu.make_async_remote_copy(
                src_ref=ready.at[w, peer, here],
                dst_ref=recv.at[w, here, pl.ds(me * ens, ens)],
                send_sem=part_send,
                recv_sem=landed,
                device_id={"mem": peer},
                device_id_type=MESH,
            ).start()
        pltpu.make_async_copy(ready.at[w, me, here], recv.at[w, here, pl.ds(me * ens, ens)], landed).start()

    def arrived(w, kind):
        here, landed = span(w, kind)
        pltpu.make_async_copy(recv.at[w, here], recv.at[w, here], landed).wait()

    def place(w):
        side, k = wave_side(w)
        return side, k, 1 - 2 * side, (STEPS - 1 - k) + side * (2 * k + lines - 2 * STEPS + 1)

    def make_ready(w, m, pair):
        for f in range(fields):
            both = jnp.concatenate([pair[0][f], pair[1][f]], axis=0).astype(jnp.bfloat16)
            for d in range(parts):
                ready[w, d, f, pl.ds(m, 16), :] = both[:, d * tile_cols : (d + 1) * tile_cols]

    def wave(w, carry):
        side, k, sign, start = place(w)
        halo_copy(side, k).wait_recv()
        lev[start] = halo[side, k].astype(jnp.float32)

        def up(level, c):
            step_row(level, start + sign * (level + 1))
            return c

        lax.fori_loop(0, STEPS - 1, up, 0)
        base = (STEPS - 1) * lines + start + sign * STEPS
        for m in range(0, ens, 16):
            make_ready(w, m, [stencil(base, m), stencil(base, m + 8)])
        part_start(w, 0)
        return carry

    def late_wave(w, kind, last=False):
        side, k, sign, start = place(w)
        toward = courant * sign.astype(jnp.float32)

        def prepare(level, c):
            base = level * lines + start + sign * (level + 1)
            for m in range(0, ens, 8):
                mid, far = ([lev[i, f, pl.ds(m, 8), :] for f in range(fields)] for i in (base, base + sign))
                for i, q in enumerate(known(mid, far, toward)):
                    partial[level, i, pl.ds(m, 8), :] = q
            return c

        lax.fori_loop(0, STEPS, prepare, 0)
        halo_copy(side, k).wait_recv()
        for m in range(0, ens, 16):
            rows16 = [halo[side, k, f, pl.ds(m, 16), :].astype(jnp.float32) for f in range(fields)]
            pair = []
            for half in range(2):
                now = [q[8 * half : 8 * half + 8] for q in rows16]
                here = pl.ds(m + 8 * half, 8)
                for level in range(STEPS):
                    if not last:
                        for f in range(fields):
                            lev[level * lines + start + sign * level, f, here, :] = now[f]
                    now = joined(now, [partial[level, i, here, :] for i in range(fields + 1)], toward)
                pair.append(now)
            make_ready(w, m, pair)
        part_start(w, kind)

    def late_loop(w, carry):
        late_wave(w, 0)
        return carry

    lax.fori_loop(0, STEPS, wave, 0)

    lax.fori_loop(STEPS, waves - LAST, late_loop, 0)
    for w in range(waves - LAST, waves):
        late_wave(w, 1, w == waves - 1)
    for w in range(waves - LAST, waves):
        part_start(w, 2)

    for load in small:
        load.wait()

    def select(w, carry):
        ids = lax.broadcasted_iota(jnp.int32, (tile_cols, slots), 0) + wave_row(w) * tile_cols
        pick[pl.ds(pl.multiple_of(w * tile_cols, tile_cols), tile_cols), :] = jnp.where(
            ids == cells[...], 1.0, 0.0
        ).astype(jnp.bfloat16)
        return carry

    lax.fori_loop(0, waves, select, 0)
    slot_ids = lax.broadcasted_iota(jnp.int32, (1, slots), 1)
    weights = jnp.where(slot_ids < count[...], 1.0 / (error[...] * error[...]), 0.0)
    chunk = 256 if slots % 256 == 0 else slots
    for s in range(0, slots, chunk):
        cut = slice(s, s + chunk)
        asked = weights[:, cut] * (values[:, cut] + error[:, cut] * noise[cut, :].T)
        for i, third in enumerate(split(asked)[:2]):
            target[i * full : (i + 1) * full, cut] = third
    line_ids = lax.broadcasted_iota(jnp.int32, (16, slots), 0)
    thirds = [q.astype(jnp.float32) for q in split(weights)]
    target[2 * full :, :] = jnp.where(
        line_ids == 0, thirds[0], jnp.where(line_ids == 1, thirds[1], jnp.where(line_ids == 2, thirds[2], 0.0))
    ).astype(jnp.bfloat16)

    def turned(a, b):
        return lax.dot_general(a, b, (((1,), (1,)), ((), ())), preferred_element_type=jnp.float32)

    chunk = 2 * tile_cols
    for c in range(0, points, chunk):
        cut = slice(c, c + chunk)
        summed = turned(target[...], pick[cut, :])
        for i, third in enumerate(split(summed[:full] + summed[full : 2 * full])[:2]):
            wanted[i * full : (i + 1) * full, cut] = third
        tail = summed[2 * full :]
        heavy[:, cut] = tail[0:1] + (tail[1:2] + tail[2:3])

    def observe(first, number):
        cut = slice(first * tile_cols, (first + number) * tile_cols)
        seen = jnp.concatenate([recv[w, 0] for w in range(first, first + number)], axis=1)
        near = seen.astype(jnp.float32)
        spread = near - jnp.sum(near, axis=0, keepdims=True) * (1.0 / full)
        wh, wm, wl = split(spread * heavy[:, cut])
        one = turned(seen, jnp.concatenate([wh, wm], axis=0))
        plain = one[:, :full] + (one[:, full:] + turned(seen, wl))
        two = turned(wanted[:, cut], seen)
        return plain, two[:full] + two[full:]

    early = waves - 1
    for w in range(early):
        arrived(w, 1 if w >= waves - LAST else 0)
    plain, aimed = observe(0, early)
    arrived(early, 1)
    plain, aimed = (a + b for a, b in zip((plain, aimed), observe(early, 1)))
    least = full - 1.0
    eye = jnp.where(
        lax.broadcasted_iota(jnp.int32, (full, full), 0) == lax.broadcasted_iota(jnp.int32, (full, full), 1), 1.0, 0.0
    )
    gram = plain - jnp.sum(plain, axis=0, keepdims=True) * (1.0 / full) + least * eye
    rhs = aimed - plain
    rhs = rhs - jnp.sum(rhs, axis=1, keepdims=True) * (1.0 / full)
    solved, eye = solve_turned(gram, rhs, least)
    mix = solved + eye
    upper = mix.astype(jnp.bfloat16)
    lower = (mix - upper.astype(jnp.float32)).astype(jnp.bfloat16)
    mix = jnp.concatenate([upper, lower], axis=1)
    for f in range(fields):
        for w in range(0, waves, 2):
            if f == 1:
                for i in (w, w + 1):
                    if i >= waves - LAST:
                        arrived(i, 2)
            block = jnp.concatenate([recv[w, f], recv[w + 1, f]], axis=1)
            done = mxu(mix, jnp.concatenate([block, block], axis=0))
            for i in range(2):
                tall[f, pl.ds(wave_row(w + i), full, stride=rows), :] = done[:, i * tile_cols : (i + 1) * tile_cols]
        out[f] = tall[f].reshape(full, rows, tile_cols).astype(jnp.bfloat16)
    pltpu.make_async_copy(edges, edges, halo_send).wait()
    gone = ready.at[:, pl.ds(0, parts - 1)]
    pltpu.make_async_copy(gone, gone, part_send).wait()


def hbm():
    return pl.BlockSpec(memory_space=pltpu.HBM)


def stay(q):
    return pltpu.with_memory_space_constraint(q, pltpu.HBM)


def body(members, obs_cells, obs_count, obs_values, obs_error, obs_noise):
    fields, ens, rows, cols = members.shape
    parts = lax.axis_size("mem")
    tile_cols = cols // parts
    full = ens * parts
    points = rows * tile_cols
    slots = obs_cells.shape[2]
    lines = rows + 2 * STEPS
    edge = pltpu.VMEM((2, STEPS, fields, ens, cols), jnp.bfloat16)
    row = pltpu.VMEM((1, slots), jnp.float32)
    dma = pltpu.SemaphoreType.DMA
    return pl.pallas_call(
        kernel,
        name="assimilate",
        out_shape=jax.ShapeDtypeStruct((fields, full, rows, tile_cols), jnp.bfloat16),
        in_specs=[hbm()] * 6,
        out_specs=pl.BlockSpec(memory_space=pltpu.VMEM),
        scratch_shapes=[
            pltpu.VMEM((STEPS * lines, fields, ens, cols), jnp.float32),
            edge,
            edge,
            pltpu.VMEM((rows, parts, fields, ens, tile_cols), jnp.bfloat16),
            pltpu.VMEM((rows, fields, full, tile_cols), jnp.bfloat16),
            pltpu.VMEM((STEPS, fields + 1, ens, cols), jnp.float32),
            pltpu.VMEM(obs_noise.shape[2:], jnp.float32),
            pltpu.VMEM((1, slots), jnp.int32),
            row,
            row,
            pltpu.VMEM((1, 1), jnp.int32),
            pltpu.VMEM((points, slots), jnp.bfloat16),
            pltpu.VMEM((2 * full + 16, slots), jnp.bfloat16),
            pltpu.VMEM((2 * full, points), jnp.bfloat16),
            pltpu.VMEM((1, points), jnp.float32),
            pltpu.VMEM((fields, full * rows, tile_cols), jnp.float32),
            dma((rows,)),
            dma((5,)),
            dma,
            dma((2, STEPS)),
            dma,
            dma((rows + LAST,)),
        ],
        compiler_params=pltpu.CompilerParams(
            vmem_limit_bytes=VMEM_BYTES, collective_id=0, has_side_effects=True
        ),
    )(stay(members), obs_count, *[stay(q) for q in (obs_cells[0], obs_values[0], obs_error[0], obs_noise[0, 0])])


def solution(mesh):
    in_specs = (
        P(None, "mem", ("tile", "grp"), None),
        P(("tile", "grp"), "mem", None),
        P(("tile", "grp"), "mem"),
        P(("tile", "grp"), "mem", None),
        P(("tile", "grp"), "mem", None),
        P(("tile", "grp"), "mem", None, None),
    )
    out_specs = P(None, None, ("tile", "grp"), "mem")
    return jax.shard_map(body, mesh=mesh, in_specs=in_specs, out_specs=out_specs, check_vma=False)
```

```python
import jax
import jax.numpy as jnp
from jax import lax
from jax.experimental import pallas as pl
from jax.experimental.pallas import tpu as pltpu
from jax.sharding import PartitionSpec as P

STEPS = 4
NEWTON_STEPS = 11
LAST = 2

courant = 0.3
gravity = 1.0
coriolis = 0.1
VMEM_BYTES = 45000000
MESH = pl.DeviceIdType.MESH


def advance(west, mid, east):
    (hw, uw, vw), (h, u, v), (he, ue, ve) = west, mid, east
    cols = h.shape[1]
    north = lambda q: pltpu.roll(q, cols - 1, 1)
    south = lambda q: pltpu.roll(q, 1, 1)
    flux = courant * (v + h * v)
    near = 0.25 * h
    rise = ue - uw
    new_h = 0.25 * (he + hw) - courant * (rise + (he * ue - hw * uw)) + (north(near - flux) + south(near + flux))
    un, us = north(u), south(u)
    new_u = (
        (ue + uw) * (0.25 - (0.5 * courant) * rise)
        - (courant * gravity) * (he - hw)
        + (0.25 * (un + us) + v * (coriolis - courant * (un - us)))
    )
    flux = courant * (0.5 * (v * v) + gravity * h)
    near = 0.25 * v
    new_v = (
        0.25 * (ve + vw)
        - u * (coriolis + courant * (ve - vw))
        + (north(near - flux) + south(near + flux))
    )
    return new_h, new_u, new_v


def known(mid, far, toward):
    (h, u, v), (hf, uf, vf) = mid, far
    cols = h.shape[1]
    north = lambda q: pltpu.roll(q, cols - 1, 1)
    south = lambda q: pltpu.roll(q, 1, 1)
    flux = courant * (v + h * v)
    near = 0.25 * h
    new_h = 0.25 * hf - toward * (uf + hf * uf) + (north(near - flux) + south(near + flux))
    un, us = north(u), south(u)
    new_u = uf * (0.25 - (0.5 * toward) * uf) - (toward * gravity) * hf
    new_u = new_u + (0.25 * (un + us) + v * (coriolis - courant * (un - us)))
    flux = courant * (0.5 * (v * v) + gravity * h)
    near = 0.25 * v
    turn = toward * u
    new_v = vf * (0.25 - turn) - coriolis * u + (north(near - flux) + south(near + flux))
    return new_h, new_u, new_v, 0.25 + turn


def joined(row, rest, toward):
    (h, u, v), (rest_h, rest_u, rest_v, turn) = row, rest
    return (
        rest_h + (0.25 * h + toward * (u + h * u)),
        rest_u + (u * (0.25 + (0.5 * toward) * u) + (toward * gravity) * h),
        rest_v + v * turn,
    )


def split(q):
    high = q.astype(jnp.bfloat16)
    rest = q - high.astype(jnp.float32)
    middle = rest.astype(jnp.bfloat16)
    return high, middle, (rest - middle.astype(jnp.float32)).astype(jnp.bfloat16)


def mxu(a, b):
    return jnp.dot(a, b, preferred_element_type=jnp.float32)


def product(a, b, fine=True):
    (ah, am, al), (bh, bm, bl) = a, b
    size = bh.shape[1]
    top = mxu(
        jnp.concatenate([ah, am], axis=1),
        jnp.concatenate([jnp.concatenate([bh, bm], axis=1)] * 2, axis=0),
    )
    if not fine:
        return top[:, :size] + top[:, size:]
    low = mxu(jnp.concatenate([ah, al], axis=1), jnp.concatenate([bl, bh], axis=0))
    return top[:, :size] + (top[:, size:] + low)


def solve_turned(gram, rhs, least):
    size = gram.shape[0]
    bound = jnp.max(jnp.sum(jnp.abs(gram), axis=0, keepdims=True), axis=1, keepdims=True)
    bound = jnp.broadcast_to(bound, (1, size))
    scale = 1.0 / bound
    eye = jnp.where(
        lax.broadcasted_iota(jnp.int32, (size, size), 0) == lax.broadcasted_iota(jnp.int32, (size, size), 1), 1.0, 0.0
    )
    low = least * scale
    mid = 1.0 + low
    gain = 4.0 / (mid * mid)
    low = gain * low
    first = split(gram)
    y = (gain * mid * scale) * gram - (gain * scale * scale) * product(first, first)
    x = (gain * mid * scale) * eye - (gain * scale * scale) * gram
    for step in range(1, NEWTON_STEPS):
        mid = 1.0 + low
        gain = 4.0 / (mid * mid)
        low = gain * low
        fine = step < NEWTON_STEPS - 4
        parts = split(y)
        if step == NEWTON_STEPS - 1:
            x = gain * (mid * x - product(split(x), parts, fine))
            break
        both = [jnp.concatenate(pair, axis=0) for pair in zip(parts, split(x))]
        done = product(both, parts, fine)
        y = gain * (mid * y - done[:size])
        x = gain * (mid * x - done[size:])
    inverse = split(x)
    found = product(split(rhs), inverse, False)
    rest = rhs - product(split(found), first)
    return found + product(split(rest), inverse, False), eye


def place_of(slab):
    groups = lax.axis_size("grp")
    return {"tile": slab // groups, "grp": lax.rem(slab, groups)}


def kernel(
    members_hbm, count_hbm, cells_hbm, values_hbm, error_hbm, noise_hbm, out,
    lev, edges, halo, ready, recv, partial, noise, cells, values, error, count, pick, target, wanted, heavy, tall,
    row_sem, load_sem, halo_send, halo_recv, part_send, part_recv,
):
    fields, ens, rows, cols = members_hbm.shape
    waves = rows
    assert rows == 2 * STEPS
    lines = rows + 2 * STEPS
    parts, tile_cols = ready.shape[1], ready.shape[4]
    full = parts * ens
    slots = cells.shape[1]
    points = rows * tile_cols
    me = lax.axis_index("mem")
    total = lax.axis_size("tile") * lax.axis_size("grp")
    slab = lax.axis_index("tile") * lax.axis_size("grp") + lax.axis_index("grp")
    after, before = lax.rem(slab + 1, total), lax.rem(slab + total - 1, total)
    peers = [lax.rem(me + p, parts) for p in range(1, parts)]
    targets = [place_of(after), place_of(before)] + [{"mem": p} for p in peers]
    quick = 1 - lax.rem(lax.axis_index("grp"), 2)
    barrier = pltpu.get_barrier_semaphore()
    for target_id in targets:
        pl.semaphore_signal(barrier, inc=1, device_id=target_id, device_id_type=MESH)

    def row_load(r):
        return pltpu.make_async_copy(members_hbm.at[:, :, r, :], lev.at[STEPS + r], row_sem.at[r])

    small = [
        pltpu.make_async_copy(src, dst, load_sem.at[i])
        for i, (src, dst) in enumerate(
            ((noise_hbm, noise), (cells_hbm, cells), (values_hbm, values), (error_hbm, error), (count_hbm, count))
        )
    ]
    for k in range(STEPS):
        row_load(rows - 1 - k).start()
        row_load(k).start()
    for load in small:
        load.start()

    def halo_copy(way, k):
        return pltpu.make_async_remote_copy(
            src_ref=edges.at[way, k],
            dst_ref=halo.at[way, k],
            send_sem=halo_send,
            recv_sem=halo_recv.at[way, k],
            device_id=place_of(after + way * (before - after)),
            device_id_type=MESH,
        )

    patient = slab == (1 - quick) + quick * (total - 2)
    for k in range(STEPS):
        for way, r in ((0, rows - 1 - k), (1, k)):
            row_load(r).wait()
            edges[way, k] = lev[STEPS + r].astype(jnp.bfloat16)
        if k == 0:
            pl.semaphore_wait(barrier, len(targets))

        @pl.when(jnp.logical_not(patient))
        def _():
            halo_copy(quick, k).start()

        halo_copy(1 - quick, k).start()

    def stencil(base, half):
        def at(i):
            return [lev[i, f, pl.ds(half, 8), :] for f in range(fields)]

        return advance(at(base - 1), at(base), at(base + 1))

    def step_row(level, line):
        base = level * lines + line
        for m in range(0, ens, 8):
            done = stencil(base, m)
            for f in range(fields):
                lev[base + lines, f, pl.ds(m, 8), :] = done[f]

    for level in range(STEPS - 1):

        def inner_row(i, carry, level=level):
            step_row(level, STEPS + level + 1 + i)
            return carry

        lax.fori_loop(0, rows - 2 * (level + 1), inner_row, 0)
        if level == 0:
            @pl.when(patient)
            def _():
                for k in range(STEPS):
                    halo_copy(quick, k).start()


    def wave_side(w):
        late = w // STEPS
        return quick + late - 2 * quick * late, lax.rem(w, STEPS)

    def wave_row(w):
        side, k = wave_side(w)
        return (STEPS - 1 - k) + side * (2 * k + 1)

    def span(w, kind):
        return pl.ds(*((0, fields), (0, 1), (1, fields - 1))[kind]), part_recv.at[w + kind // 2 * LAST]

    def part_start(w, kind):
        here, landed = span(w, kind)
        for peer in peers:
            pltpu.make_async_remote_copy(
                src_ref=ready.at[w, peer, here],
                dst_ref=recv.at[w, here, pl.ds(me * ens, ens)],
                send_sem=part_send,
                recv_sem=landed,
                device_id={"mem": peer},
                device_id_type=MESH,
            ).start()
        pltpu.make_async_copy(ready.at[w, me, here], recv.at[w, here, pl.ds(me * ens, ens)], landed).start()

    def arrived(w, kind):
        here, landed = span(w, kind)
        pltpu.make_async_copy(recv.at[w, here], recv.at[w, here], landed).wait()

    def place(w):
        side, k = wave_side(w)
        return side, k, 1 - 2 * side, (STEPS - 1 - k) + side * (2 * k + lines - 2 * STEPS + 1)

    def make_ready(w, m, pair):
        for f in range(fields):
            both = jnp.concatenate([pair[0][f], pair[1][f]], axis=0).astype(jnp.bfloat16)
            for d in range(parts):
                ready[w, d, f, pl.ds(m, 16), :] = both[:, d * tile_cols : (d + 1) * tile_cols]

    def wave(w, carry):
        side, k, sign, start = place(w)
        halo_copy(side, k).wait_recv()
        lev[start] = halo[side, k].astype(jnp.float32)

        def up(level, c):
            step_row(level, start + sign * (level + 1))
            return c

        lax.fori_loop(0, STEPS - 1, up, 0)
        base = (STEPS - 1) * lines + start + sign * STEPS
        for m in range(0, ens, 16):
            make_ready(w, m, [stencil(base, m), stencil(base, m + 8)])
        part_start(w, 0)
        return carry

    def late_wave(w, kind, last=False):
        side, k, sign, start = place(w)
        toward = courant * sign.astype(jnp.float32)

        def prepare(level, c):
            base = level * lines + start + sign * (level + 1)
            for m in range(0, ens, 8):
                mid, far = ([lev[i, f, pl.ds(m, 8), :] for f in range(fields)] for i in (base, base + sign))
                for i, q in enumerate(known(mid, far, toward)):
                    partial[level, i, pl.ds(m, 8), :] = q
            return c

        lax.fori_loop(0, STEPS, prepare, 0)
        halo_copy(side, k).wait_recv()
        for m in range(0, ens, 16):
            rows16 = [halo[side, k, f, pl.ds(m, 16), :].astype(jnp.float32) for f in range(fields)]
            pair = []
            for half in range(2):
                now = [q[8 * half : 8 * half + 8] for q in rows16]
                here = pl.ds(m + 8 * half, 8)
                for level in range(STEPS):
                    if not last:
                        for f in range(fields):
                            lev[level * lines + start + sign * level, f, here, :] = now[f]
                    now = joined(now, [partial[level, i, here, :] for i in range(fields + 1)], toward)
                pair.append(now)
            make_ready(w, m, pair)
        part_start(w, kind)

    def late_loop(w, carry):
        late_wave(w, 0)
        return carry

    lax.fori_loop(0, STEPS, wave, 0)

    lax.fori_loop(STEPS, waves - LAST, late_loop, 0)
    for w in range(waves - LAST, waves):
        late_wave(w, 1, w == waves - 1)
    for w in range(waves - LAST, waves):
        part_start(w, 2)

    for load in small:
        load.wait()

    def select(w, carry):
        ids = lax.broadcasted_iota(jnp.int32, (tile_cols, slots), 0) + wave_row(w) * tile_cols
        pick[pl.ds(pl.multiple_of(w * tile_cols, tile_cols), tile_cols), :] = jnp.where(
            ids == cells[...], 1.0, 0.0
        ).astype(jnp.bfloat16)
        return carry

    lax.fori_loop(0, waves, select, 0)
    slot_ids = lax.broadcasted_iota(jnp.int32, (1, slots), 1)
    weights = jnp.where(slot_ids < count[...], 1.0 / (error[...] * error[...]), 0.0)
    chunk = 256 if slots % 256 == 0 else slots
    for s in range(0, slots, chunk):
        cut = slice(s, s + chunk)
        asked = weights[:, cut] * (values[:, cut] + error[:, cut] * noise[cut, :].T)
        for i, third in enumerate(split(asked)[:2]):
            target[i * full : (i + 1) * full, cut] = third
    line_ids = lax.broadcasted_iota(jnp.int32, (16, slots), 0)
    thirds = [q.astype(jnp.float32) for q in split(weights)]
    target[2 * full :, :] = jnp.where(
        line_ids == 0, thirds[0], jnp.where(line_ids == 1, thirds[1], jnp.where(line_ids == 2, thirds[2], 0.0))
    ).astype(jnp.bfloat16)

    def turned(a, b):
        return lax.dot_general(a, b, (((1,), (1,)), ((), ())), preferred_element_type=jnp.float32)

    chunk = 2 * tile_cols
    for c in range(0, points, chunk):
        cut = slice(c, c + chunk)
        summed = turned(target[...], pick[cut, :])
        for i, third in enumerate(split(summed[:full] + summed[full : 2 * full])[:2]):
            wanted[i * full : (i + 1) * full, cut] = third
        tail = summed[2 * full :]
        heavy[:, cut] = tail[0:1] + (tail[1:2] + tail[2:3])

    def observe(first, number):
        cut = slice(first * tile_cols, (first + number) * tile_cols)
        seen = jnp.concatenate([recv[w, 0] for w in range(first, first + number)], axis=1)
        near = seen.astype(jnp.float32)
        spread = near - jnp.sum(near, axis=0, keepdims=True) * (1.0 / full)
        wh, wm, wl = split(spread * heavy[:, cut])
        one = turned(seen, jnp.concatenate([wh, wm], axis=0))
        plain = one[:, :full] + (one[:, full:] + turned(seen, wl))
        two = turned(wanted[:, cut], seen)
        return plain, two[:full] + two[full:]

    early = waves - 1
    for w in range(early):
        arrived(w, 1 if w >= waves - LAST else 0)
    plain, aimed = observe(0, early)
    arrived(early, 1)
    plain, aimed = (a + b for a, b in zip((plain, aimed), observe(early, 1)))
    least = full - 1.0
    eye = jnp.where(
        lax.broadcasted_iota(jnp.int32, (full, full), 0) == lax.broadcasted_iota(jnp.int32, (full, full), 1), 1.0, 0.0
    )
    gram = plain - jnp.sum(plain, axis=0, keepdims=True) * (1.0 / full) + least * eye
    rhs = aimed - plain
    rhs = rhs - jnp.sum(rhs, axis=1, keepdims=True) * (1.0 / full)
    solved, eye = solve_turned(gram, rhs, least)
    mix = solved + eye
    upper = mix.astype(jnp.bfloat16)
    lower = (mix - upper.astype(jnp.float32)).astype(jnp.bfloat16)
    mix = jnp.concatenate([upper, lower], axis=1)
    for f in range(fields):
        for w in range(0, waves, 2):
            if f == 1:
                for i in (w, w + 1):
                    if i >= waves - LAST:
                        arrived(i, 2)
            block = jnp.concatenate([recv[w, f], recv[w + 1, f]], axis=1)
            done = mxu(mix, jnp.concatenate([block, block], axis=0))
            for i in range(2):
                tall[f, pl.ds(wave_row(w + i), full, stride=rows), :] = done[:, i * tile_cols : (i + 1) * tile_cols]
        out[f] = tall[f].reshape(full, rows, tile_cols).astype(jnp.bfloat16)
    pltpu.make_async_copy(edges, edges, halo_send).wait()
    gone = ready.at[:, pl.ds(0, parts - 1)]
    pltpu.make_async_copy(gone, gone, part_send).wait()


def hbm():
    return pl.BlockSpec(memory_space=pltpu.HBM)


def stay(q):
    return pltpu.with_memory_space_constraint(q, pltpu.HBM)


def body(members, obs_cells, obs_count, obs_values, obs_error, obs_noise):
    fields, ens, rows, cols = members.shape
    parts = lax.axis_size("mem")
    tile_cols = cols // parts
    full = ens * parts
    points = rows * tile_cols
    slots = obs_cells.shape[2]
    lines = rows + 2 * STEPS
    edge = pltpu.VMEM((2, STEPS, fields, ens, cols), jnp.bfloat16)
    row = pltpu.VMEM((1, slots), jnp.float32)
    dma = pltpu.SemaphoreType.DMA
    return pl.pallas_call(
        kernel,
        name="assimilate",
        out_shape=jax.ShapeDtypeStruct((fields, full, rows, tile_cols), jnp.bfloat16),
        in_specs=[hbm()] * 6,
        out_specs=pl.BlockSpec(memory_space=pltpu.VMEM),
        scratch_shapes=[
            pltpu.VMEM((STEPS * lines, fields, ens, cols), jnp.float32),
            edge,
            edge,
            pltpu.VMEM((rows, parts, fields, ens, tile_cols), jnp.bfloat16),
            pltpu.VMEM((rows, fields, full, tile_cols), jnp.bfloat16),
            pltpu.VMEM((STEPS, fields + 1, ens, cols), jnp.float32),
            pltpu.VMEM(obs_noise.shape[2:], jnp.float32),
            pltpu.VMEM((1, slots), jnp.int32),
            row,
            row,
            pltpu.VMEM((1, 1), jnp.int32),
            pltpu.VMEM((points, slots), jnp.bfloat16),
            pltpu.VMEM((2 * full + 16, slots), jnp.bfloat16),
            pltpu.VMEM((2 * full, points), jnp.bfloat16),
            pltpu.VMEM((1, points), jnp.float32),
            pltpu.VMEM((fields, full * rows, tile_cols), jnp.float32),
            dma((rows,)),
            dma((5,)),
            dma,
            dma((2, STEPS)),
            dma,
            dma((rows + LAST,)),
        ],
        compiler_params=pltpu.CompilerParams(
            vmem_limit_bytes=VMEM_BYTES, collective_id=0, has_side_effects=True
        ),
    )(stay(members), obs_count, *[stay(q) for q in (obs_cells[0], obs_values[0], obs_error[0], obs_noise[0, 0])])


def solution(mesh):
    in_specs = (
        P(None, "mem", ("tile", "grp"), None),
        P(("tile", "grp"), "mem", None),
        P(("tile", "grp"), "mem"),
        P(("tile", "grp"), "mem", None),
        P(("tile", "grp"), "mem", None),
        P(("tile", "grp"), "mem", None, None),
    )
    out_specs = P(None, None, ("tile", "grp"), "mem")
    return jax.shard_map(body, mesh=mesh, in_specs=in_specs, out_specs=out_specs, check_vma=False)
```

```python
import jax
import jax.numpy as jnp
from jax import lax
from jax.experimental import pallas as pl
from jax.experimental.pallas import tpu as pltpu
from jax.sharding import PartitionSpec as P

STEPS = 4
NEWTON_STEPS = 11
LAST = 2

courant = 0.3
gravity = 1.0
coriolis = 0.1
VMEM_BYTES = 45000000
MESH = pl.DeviceIdType.MESH


def advance(west, mid, east):
    (hw, uw, vw), (h, u, v), (he, ue, ve) = west, mid, east
    cols = h.shape[1]
    north = lambda q: pltpu.roll(q, cols - 1, 1)
    south = lambda q: pltpu.roll(q, 1, 1)
    flux = courant * (v + h * v)
    near = 0.25 * h
    rise = ue - uw
    new_h = 0.25 * (he + hw) - courant * (rise + (he * ue - hw * uw)) + (north(near - flux) + south(near + flux))
    un, us = north(u), south(u)
    new_u = (
        (ue + uw) * (0.25 - (0.5 * courant) * rise)
        - (courant * gravity) * (he - hw)
        + (0.25 * (un + us) + v * (coriolis - courant * (un - us)))
    )
    flux = courant * (0.5 * (v * v) + gravity * h)
    near = 0.25 * v
    new_v = (
        0.25 * (ve + vw)
        - u * (coriolis + courant * (ve - vw))
        + (north(near - flux) + south(near + flux))
    )
    return new_h, new_u, new_v


def known(mid, far, toward):
    (h, u, v), (hf, uf, vf) = mid, far
    cols = h.shape[1]
    north = lambda q: pltpu.roll(q, cols - 1, 1)
    south = lambda q: pltpu.roll(q, 1, 1)
    flux = courant * (v + h * v)
    near = 0.25 * h
    new_h = 0.25 * hf - toward * (uf + hf * uf) + (north(near - flux) + south(near + flux))
    un, us = north(u), south(u)
    new_u = uf * (0.25 - (0.5 * toward) * uf) - (toward * gravity) * hf
    new_u = new_u + (0.25 * (un + us) + v * (coriolis - courant * (un - us)))
    flux = courant * (0.5 * (v * v) + gravity * h)
    near = 0.25 * v
    turn = toward * u
    new_v = vf * (0.25 - turn) - coriolis * u + (north(near - flux) + south(near + flux))
    return new_h, new_u, new_v, 0.25 + turn


def joined(row, rest, toward):
    (h, u, v), (rest_h, rest_u, rest_v, turn) = row, rest
    return (
        rest_h + (0.25 * h + toward * (u + h * u)),
        rest_u + (u * (0.25 + (0.5 * toward) * u) + (toward * gravity) * h),
        rest_v + v * turn,
    )


def split(q):
    high = q.astype(jnp.bfloat16)
    rest = q - high.astype(jnp.float32)
    middle = rest.astype(jnp.bfloat16)
    return high, middle, (rest - middle.astype(jnp.float32)).astype(jnp.bfloat16)


def mxu(a, b):
    return jnp.dot(a, b, preferred_element_type=jnp.float32)


def product(a, b, fine=True):
    (ah, am, al), (bh, bm, bl) = a, b
    size = bh.shape[1]
    top = mxu(
        jnp.concatenate([ah, am], axis=1),
        jnp.concatenate([jnp.concatenate([bh, bm], axis=1)] * 2, axis=0),
    )
    if not fine:
        return top[:, :size] + top[:, size:]
    low = mxu(jnp.concatenate([ah, al], axis=1), jnp.concatenate([bl, bh], axis=0))
    return top[:, :size] + (top[:, size:] + low)


def solve_turned(gram, rhs, least):
    size = gram.shape[0]
    bound = jnp.max(jnp.sum(jnp.abs(gram), axis=0, keepdims=True), axis=1, keepdims=True)
    bound = jnp.broadcast_to(bound, (1, size))
    scale = 1.0 / bound
    eye = jnp.where(
        lax.broadcasted_iota(jnp.int32, (size, size), 0) == lax.broadcasted_iota(jnp.int32, (size, size), 1), 1.0, 0.0
    )
    low = least * scale
    mid = 1.0 + low
    gain = 4.0 / (mid * mid)
    low = gain * low
    first = split(gram)
    y = (gain * mid * scale) * gram - (gain * scale * scale) * product(first, first)
    x = (gain * mid * scale) * eye - (gain * scale * scale) * gram
    for step in range(1, NEWTON_STEPS):
        mid = 1.0 + low
        gain = 4.0 / (mid * mid)
        low = gain * low
        fine = step < NEWTON_STEPS - 4
        parts = split(y)
        if step == NEWTON_STEPS - 1:
            x = gain * (mid * x - product(split(x), parts, fine))
            break
        both = [jnp.concatenate(pair, axis=0) for pair in zip(parts, split(x))]
        done = product(both, parts, fine)
        y = gain * (mid * y - done[:size])
        x = gain * (mid * x - done[size:])
    inverse = split(x)
    found = product(split(rhs), inverse, False)
    rest = rhs - product(split(found), first)
    return found + product(split(rest), inverse, False), eye


def place_of(slab):
    groups = lax.axis_size("grp")
    return {"tile": slab // groups, "grp": lax.rem(slab, groups)}


def kernel(
    members_hbm, count_hbm, cells_hbm, values_hbm, error_hbm, noise_hbm, out,
    lev, edges, halo, ready, recv, partial, noise, cells, values, error, count, pick, target, wanted, heavy, tall,
    row_sem, load_sem, halo_send, halo_recv, part_send, part_recv,
):
    fields, ens, rows, cols = members_hbm.shape
    waves = rows
    assert rows == 2 * STEPS
    lines = rows + 2 * STEPS
    parts, tile_cols = ready.shape[1], ready.shape[4]
    full = parts * ens
    slots = cells.shape[1]
    points = rows * tile_cols
    me = lax.axis_index("mem")
    total = lax.axis_size("tile") * lax.axis_size("grp")
    slab = lax.axis_index("tile") * lax.axis_size("grp") + lax.axis_index("grp")
    after, before = lax.rem(slab + 1, total), lax.rem(slab + total - 1, total)
    peers = [lax.rem(me + p, parts) for p in range(1, parts)]
    targets = [place_of(after), place_of(before)] + [{"mem": p} for p in peers]
    quick = 1 - lax.rem(lax.axis_index("grp"), 2)
    barrier = pltpu.get_barrier_semaphore()
    for target_id in targets:
        pl.semaphore_signal(barrier, inc=1, device_id=target_id, device_id_type=MESH)

    def row_load(r):
        return pltpu.make_async_copy(members_hbm.at[:, :, r, :], lev.at[STEPS + r], row_sem.at[r])

    small = [
        pltpu.make_async_copy(src, dst, load_sem.at[i])
        for i, (src, dst) in enumerate(
            ((noise_hbm, noise), (cells_hbm, cells), (values_hbm, values), (error_hbm, error), (count_hbm, count))
        )
    ]
    for k in range(STEPS):
        row_load(rows - 1 - k).start()
        row_load(k).start()
    for load in small:
        load.start()

    def halo_copy(way, k):
        return pltpu.make_async_remote_copy(
            src_ref=edges.at[way, k],
            dst_ref=halo.at[way, k],
            send_sem=halo_send,
            recv_sem=halo_recv.at[way, k],
            device_id=place_of(after + way * (before - after)),
            device_id_type=MESH,
        )

    patient = slab == (1 - quick) + quick * (total - 2)
    for k in range(STEPS):
        for way, r in ((0, rows - 1 - k), (1, k)):
            row_load(r).wait()
            edges[way, k] = lev[STEPS + r].astype(jnp.bfloat16)
        if k == 0:
            pl.semaphore_wait(barrier, len(targets))

        @pl.when(jnp.logical_not(patient))
        def _():
            halo_copy(quick, k).start()

        halo_copy(1 - quick, k).start()

    def stencil(base, half):
        def at(i):
            return [lev[i, f, pl.ds(half, 8), :] for f in range(fields)]

        return advance(at(base - 1), at(base), at(base + 1))

    def step_row(level, line):
        base = level * lines + line
        for m in range(0, ens, 8):
            done = stencil(base, m)
            for f in range(fields):
                lev[base + lines, f, pl.ds(m, 8), :] = done[f]

    for level in range(STEPS - 1):

        def inner_row(i, carry, level=level):
            step_row(level, STEPS + level + 1 + i)
            return carry

        lax.fori_loop(0, rows - 2 * (level + 1), inner_row, 0)
        if level == 0:
            @pl.when(patient)
            def _():
                for k in range(STEPS):
                    halo_copy(quick, k).start()


    def wave_side(w):
        late = w // STEPS
        return quick + late - 2 * quick * late, lax.rem(w, STEPS)

    def wave_row(w):
        side, k = wave_side(w)
        return (STEPS - 1 - k) + side * (2 * k + 1)

    def span(w, kind):
        return pl.ds(*((0, fields), (0, 1), (1, fields - 1))[kind]), part_recv.at[w + kind // 2 * LAST]

    def part_start(w, kind):
        here, landed = span(w, kind)
        for peer in peers:
            pltpu.make_async_remote_copy(
                src_ref=ready.at[w, peer, here],
                dst_ref=recv.at[w, here, pl.ds(me * ens, ens)],
                send_sem=part_send,
                recv_sem=landed,
                device_id={"mem": peer},
                device_id_type=MESH,
            ).start()
        pltpu.make_async_copy(ready.at[w, me, here], recv.at[w, here, pl.ds(me * ens, ens)], landed).start()

    def arrived(w, kind):
        here, landed = span(w, kind)
        pltpu.make_async_copy(recv.at[w, here], recv.at[w, here], landed).wait()

    def place(w):
        side, k = wave_side(w)
        return side, k, 1 - 2 * side, (STEPS - 1 - k) + side * (2 * k + lines - 2 * STEPS + 1)

    def make_ready(w, m, pair, some=None):
        for i, f in enumerate(range(fields) if some is None else some):
            both = jnp.concatenate([pair[0][i], pair[1][i]], axis=0).astype(jnp.bfloat16)
            for d in range(parts):
                ready[w, d, f, pl.ds(m, 16), :] = both[:, d * tile_cols : (d + 1) * tile_cols]

    def wave(w, carry):
        side, k, sign, start = place(w)
        halo_copy(side, k).wait_recv()
        lev[start] = halo[side, k].astype(jnp.float32)

        def up(level, c):
            step_row(level, start + sign * (level + 1))
            return c

        lax.fori_loop(0, STEPS - 1, up, 0)
        base = (STEPS - 1) * lines + start + sign * STEPS
        for m in range(0, ens, 16):
            make_ready(w, m, [stencil(base, m), stencil(base, m + 8)])
        part_start(w, 0)
        return carry

    def late_wave(w, kind, last=False):
        side, k, sign, start = place(w)
        toward = courant * sign.astype(jnp.float32)

        def prepare(level, c):
            base = level * lines + start + sign * (level + 1)
            for m in range(0, ens, 8):
                mid, far = ([lev[i, f, pl.ds(m, 8), :] for f in range(fields)] for i in (base, base + sign))
                for i, q in enumerate(known(mid, far, toward)):
                    partial[level, i, pl.ds(m, 8), :] = q
            return c

        lax.fori_loop(0, STEPS, prepare, 0)
        halo_copy(side, k).wait_recv()
        rests = []
        for m in range(0, ens, 16):
            rows16 = [halo[side, k, f, pl.ds(m, 16), :].astype(jnp.float32) for f in range(fields)]
            pair = []
            for half in range(2):
                now = [q[8 * half : 8 * half + 8] for q in rows16]
                here = pl.ds(m + 8 * half, 8)
                for level in range(STEPS):
                    if not last:
                        for f in range(fields):
                            lev[level * lines + start + sign * level, f, here, :] = now[f]
                    now = joined(now, [partial[level, i, here, :] for i in range(fields + 1)], toward)
                pair.append(now)
            if last:
                make_ready(w, m, [q[:1] for q in pair], (0,))
                rests.append([q[1:] for q in pair])
            else:
                make_ready(w, m, pair)
        part_start(w, kind)
        for i, pair in enumerate(rests):
            make_ready(w, 16 * i, pair, (1, 2))

    def late_loop(w, carry):
        late_wave(w, 0)
        return carry

    lax.fori_loop(0, STEPS, wave, 0)

    lax.fori_loop(STEPS, waves - LAST, late_loop, 0)
    for w in range(waves - LAST, waves):
        late_wave(w, 1, w == waves - 1)
    for w in range(waves - LAST, waves):
        part_start(w, 2)

    for load in small:
        load.wait()

    def select(w, carry):
        ids = lax.broadcasted_iota(jnp.int32, (tile_cols, slots), 0) + wave_row(w) * tile_cols
        pick[pl.ds(pl.multiple_of(w * tile_cols, tile_cols), tile_cols), :] = jnp.where(
            ids == cells[...], 1.0, 0.0
        ).astype(jnp.bfloat16)
        return carry

    lax.fori_loop(0, waves, select, 0)
    slot_ids = lax.broadcasted_iota(jnp.int32, (1, slots), 1)
    weights = jnp.where(slot_ids < count[...], 1.0 / (error[...] * error[...]), 0.0)
    chunk = 256 if slots % 256 == 0 else slots
    for s in range(0, slots, chunk):
        cut = slice(s, s + chunk)
        asked = weights[:, cut] * (values[:, cut] + error[:, cut] * noise[cut, :].T)
        for i, third in enumerate(split(asked)[:2]):
            target[i * full : (i + 1) * full, cut] = third
    line_ids = lax.broadcasted_iota(jnp.int32, (16, slots), 0)
    thirds = [q.astype(jnp.float32) for q in split(weights)]
    target[2 * full :, :] = jnp.where(
        line_ids == 0, thirds[0], jnp.where(line_ids == 1, thirds[1], jnp.where(line_ids == 2, thirds[2], 0.0))
    ).astype(jnp.bfloat16)

    def turned(a, b):
        return lax.dot_general(a, b, (((1,), (1,)), ((), ())), preferred_element_type=jnp.float32)

    chunk = 2 * tile_cols
    for c in range(0, points, chunk):
        cut = slice(c, c + chunk)
        summed = turned(target[...], pick[cut, :])
        for i, third in enumerate(split(summed[:full] + summed[full : 2 * full])[:2]):
            wanted[i * full : (i + 1) * full, cut] = third
        tail = summed[2 * full :]
        heavy[:, cut] = tail[0:1] + (tail[1:2] + tail[2:3])

    def observe(first, number):
        cut = slice(first * tile_cols, (first + number) * tile_cols)
        seen = jnp.concatenate([recv[w, 0] for w in range(first, first + number)], axis=1)
        near = seen.astype(jnp.float32)
        spread = near - jnp.sum(near, axis=0, keepdims=True) * (1.0 / full)
        wh, wm, wl = split(spread * heavy[:, cut])
        one = turned(seen, jnp.concatenate([wh, wm], axis=0))
        plain = one[:, :full] + (one[:, full:] + turned(seen, wl))
        two = turned(wanted[:, cut], seen)
        return plain, two[:full] + two[full:]

    early = waves - 1
    for w in range(early):
        arrived(w, 1 if w >= waves - LAST else 0)
    plain, aimed = observe(0, early)
    arrived(early, 1)
    plain, aimed = (a + b for a, b in zip((plain, aimed), observe(early, 1)))
    least = full - 1.0
    eye = jnp.where(
        lax.broadcasted_iota(jnp.int32, (full, full), 0) == lax.broadcasted_iota(jnp.int32, (full, full), 1), 1.0, 0.0
    )
    gram = plain - jnp.sum(plain, axis=0, keepdims=True) * (1.0 / full) + least * eye
    rhs = aimed - plain
    rhs = rhs - jnp.sum(rhs, axis=1, keepdims=True) * (1.0 / full)
    solved, eye = solve_turned(gram, rhs, least)
    mix = solved + eye
    upper = mix.astype(jnp.bfloat16)
    lower = (mix - upper.astype(jnp.float32)).astype(jnp.bfloat16)
    mix = jnp.concatenate([upper, lower], axis=1)
    for f in range(fields):
        for w in range(0, waves, 2):
            if f == 1:
                for i in (w, w + 1):
                    if i >= waves - LAST:
                        arrived(i, 2)
            block = jnp.concatenate([recv[w, f], recv[w + 1, f]], axis=1)
            done = mxu(mix, jnp.concatenate([block, block], axis=0))
            for i in range(2):
                tall[f, pl.ds(wave_row(w + i), full, stride=rows), :] = done[:, i * tile_cols : (i + 1) * tile_cols]
        out[f] = tall[f].reshape(full, rows, tile_cols).astype(jnp.bfloat16)
    pltpu.make_async_copy(edges, edges, halo_send).wait()
    gone = ready.at[:, pl.ds(0, parts - 1)]
    pltpu.make_async_copy(gone, gone, part_send).wait()


def hbm():
    return pl.BlockSpec(memory_space=pltpu.HBM)


def stay(q):
    return pltpu.with_memory_space_constraint(q, pltpu.HBM)


def body(members, obs_cells, obs_count, obs_values, obs_error, obs_noise):
    fields, ens, rows, cols = members.shape
    parts = lax.axis_size("mem")
    tile_cols = cols // parts
    full = ens * parts
    points = rows * tile_cols
    slots = obs_cells.shape[2]
    lines = rows + 2 * STEPS
    edge = pltpu.VMEM((2, STEPS, fields, ens, cols), jnp.bfloat16)
    row = pltpu.VMEM((1, slots), jnp.float32)
    dma = pltpu.SemaphoreType.DMA
    return pl.pallas_call(
        kernel,
        name="assimilate",
        out_shape=jax.ShapeDtypeStruct((fields, full, rows, tile_cols), jnp.bfloat16),
        in_specs=[hbm()] * 6,
        out_specs=pl.BlockSpec(memory_space=pltpu.VMEM),
        scratch_shapes=[
            pltpu.VMEM((STEPS * lines, fields, ens, cols), jnp.float32),
            edge,
            edge,
            pltpu.VMEM((rows, parts, fields, ens, tile_cols), jnp.bfloat16),
            pltpu.VMEM((rows, fields, full, tile_cols), jnp.bfloat16),
            pltpu.VMEM((STEPS, fields + 1, ens, cols), jnp.float32),
            pltpu.VMEM(obs_noise.shape[2:], jnp.float32),
            pltpu.VMEM((1, slots), jnp.int32),
            row,
            row,
            pltpu.VMEM((1, 1), jnp.int32),
            pltpu.VMEM((points, slots), jnp.bfloat16),
            pltpu.VMEM((2 * full + 16, slots), jnp.bfloat16),
            pltpu.VMEM((2 * full, points), jnp.bfloat16),
            pltpu.VMEM((1, points), jnp.float32),
            pltpu.VMEM((fields, full * rows, tile_cols), jnp.float32),
            dma((rows,)),
            dma((5,)),
            dma,
            dma((2, STEPS)),
            dma,
            dma((rows + LAST,)),
        ],
        compiler_params=pltpu.CompilerParams(
            vmem_limit_bytes=VMEM_BYTES, collective_id=0, has_side_effects=True
        ),
    )(stay(members), obs_count, *[stay(q) for q in (obs_cells[0], obs_values[0], obs_error[0], obs_noise[0, 0])])


def solution(mesh):
    in_specs = (
        P(None, "mem", ("tile", "grp"), None),
        P(("tile", "grp"), "mem", None),
        P(("tile", "grp"), "mem"),
        P(("tile", "grp"), "mem", None),
        P(("tile", "grp"), "mem", None),
        P(("tile", "grp"), "mem", None, None),
    )
    out_specs = P(None, None, ("tile", "grp"), "mem")
    return jax.shard_map(body, mesh=mesh, in_specs=in_specs, out_specs=out_specs, check_vma=False)
```

```python
import jax
import jax.numpy as jnp
from jax import lax
from jax.experimental import pallas as pl
from jax.experimental.pallas import tpu as pltpu
from jax.sharding import PartitionSpec as P

STEPS = 4
NEWTON_STEPS = 11
LAST = 2

courant = 0.3
gravity = 1.0
coriolis = 0.1
VMEM_BYTES = 45000000
MESH = pl.DeviceIdType.MESH


def advance(west, mid, east):
    (hw, uw, vw), (h, u, v), (he, ue, ve) = west, mid, east
    cols = h.shape[1]
    north = lambda q: pltpu.roll(q, cols - 1, 1)
    south = lambda q: pltpu.roll(q, 1, 1)
    flux = courant * (v + h * v)
    near = 0.25 * h
    rise = ue - uw
    new_h = 0.25 * (he + hw) - courant * (rise + (he * ue - hw * uw)) + (north(near - flux) + south(near + flux))
    un, us = north(u), south(u)
    new_u = (
        (ue + uw) * (0.25 - (0.5 * courant) * rise)
        - (courant * gravity) * (he - hw)
        + (0.25 * (un + us) + v * (coriolis - courant * (un - us)))
    )
    flux = courant * (0.5 * (v * v) + gravity * h)
    near = 0.25 * v
    new_v = (
        0.25 * (ve + vw)
        - u * (coriolis + courant * (ve - vw))
        + (north(near - flux) + south(near + flux))
    )
    return new_h, new_u, new_v


def known(mid, far, toward):
    (h, u, v), (hf, uf, vf) = mid, far
    cols = h.shape[1]
    north = lambda q: pltpu.roll(q, cols - 1, 1)
    south = lambda q: pltpu.roll(q, 1, 1)
    flux = courant * (v + h * v)
    near = 0.25 * h
    new_h = 0.25 * hf - toward * (uf + hf * uf) + (north(near - flux) + south(near + flux))
    un, us = north(u), south(u)
    new_u = uf * (0.25 - (0.5 * toward) * uf) - (toward * gravity) * hf
    new_u = new_u + (0.25 * (un + us) + v * (coriolis - courant * (un - us)))
    flux = courant * (0.5 * (v * v) + gravity * h)
    near = 0.25 * v
    turn = toward * u
    new_v = vf * (0.25 - turn) - coriolis * u + (north(near - flux) + south(near + flux))
    return new_h, new_u, new_v, 0.25 + turn


def joined(row, rest, toward):
    (h, u, v), (rest_h, rest_u, rest_v, turn) = row, rest
    return (
        rest_h + (0.25 * h + toward * (u + h * u)),
        rest_u + (u * (0.25 + (0.5 * toward) * u) + (toward * gravity) * h),
        rest_v + v * turn,
    )


def split(q):
    high = q.astype(jnp.bfloat16)
    rest = q - high.astype(jnp.float32)
    middle = rest.astype(jnp.bfloat16)
    return high, middle, (rest - middle.astype(jnp.float32)).astype(jnp.bfloat16)


def mxu(a, b):
    return jnp.dot(a, b, preferred_element_type=jnp.float32)


def product(a, b, fine=True):
    (ah, am, al), (bh, bm, bl) = a, b
    size = bh.shape[1]
    top = mxu(
        jnp.concatenate([ah, am], axis=1),
        jnp.concatenate([jnp.concatenate([bh, bm], axis=1)] * 2, axis=0),
    )
    if not fine:
        return top[:, :size] + top[:, size:]
    low = mxu(jnp.concatenate([ah, al], axis=1), jnp.concatenate([bl, bh], axis=0))
    return top[:, :size] + (top[:, size:] + low)


def solve_turned(gram, rhs, least):
    size = gram.shape[0]
    bound = jnp.max(jnp.sum(jnp.abs(gram), axis=0, keepdims=True), axis=1, keepdims=True)
    bound = jnp.broadcast_to(bound, (1, size))
    scale = 1.0 / bound
    eye = jnp.where(
        lax.broadcasted_iota(jnp.int32, (size, size), 0) == lax.broadcasted_iota(jnp.int32, (size, size), 1), 1.0, 0.0
    )
    low = least * scale
    mid = 1.0 + low
    gain = 4.0 / (mid * mid)
    low = gain * low
    first = split(gram)
    y = (gain * mid * scale) * gram - (gain * scale * scale) * product(first, first)
    x = (gain * mid * scale) * eye - (gain * scale * scale) * gram
    for step in range(1, NEWTON_STEPS):
        mid = 1.0 + low
        gain = 4.0 / (mid * mid)
        low = gain * low
        fine = step < NEWTON_STEPS - 4
        parts = split(y)
        if step == NEWTON_STEPS - 1:
            x = gain * (mid * x - product(split(x), parts, fine))
            break
        y, x = gain * (mid * y - product(parts, parts, fine)), gain * (mid * x - product(split(x), parts, fine))
    inverse = split(x)
    found = product(split(rhs), inverse, False)
    rest = rhs - product(split(found), first)
    return found + product(split(rest), inverse, False), eye


def place_of(slab):
    groups = lax.axis_size("grp")
    return {"tile": slab // groups, "grp": lax.rem(slab, groups)}


def kernel(
    members_hbm, count_hbm, cells_hbm, values_hbm, error_hbm, noise_hbm, out,
    lev, edges, halo, ready, recv, partial, noise, cells, values, error, count, pick, target, wanted, heavy, tall,
    row_sem, load_sem, halo_send, halo_recv, part_send, part_recv,
):
    fields, ens, rows, cols = members_hbm.shape
    waves = rows
    assert rows == 2 * STEPS
    lines = rows + 2 * STEPS
    parts, tile_cols = ready.shape[1], ready.shape[4]
    full = parts * ens
    slots = cells.shape[1]
    points = rows * tile_cols
    me = lax.axis_index("mem")
    total = lax.axis_size("tile") * lax.axis_size("grp")
    slab = lax.axis_index("tile") * lax.axis_size("grp") + lax.axis_index("grp")
    after, before = lax.rem(slab + 1, total), lax.rem(slab + total - 1, total)
    peers = [lax.rem(me + p, parts) for p in range(1, parts)]
    targets = [place_of(after), place_of(before)] + [{"mem": p} for p in peers]
    quick = 1 - lax.rem(lax.axis_index("grp"), 2)
    barrier = pltpu.get_barrier_semaphore()
    for target_id in targets:
        pl.semaphore_signal(barrier, inc=1, device_id=target_id, device_id_type=MESH)

    def row_load(r):
        return pltpu.make_async_copy(members_hbm.at[:, :, r, :], lev.at[STEPS + r], row_sem.at[r])

    small = [
        pltpu.make_async_copy(src, dst, load_sem.at[i])
        for i, (src, dst) in enumerate(
            ((noise_hbm, noise), (cells_hbm, cells), (values_hbm, values), (error_hbm, error), (count_hbm, count))
        )
    ]
    for k in range(STEPS):
        row_load(rows - 1 - k).start()
        row_load(k).start()
    for load in small:
        load.start()

    def halo_copy(way, k):
        return pltpu.make_async_remote_copy(
            src_ref=edges.at[way, k],
            dst_ref=halo.at[way, k],
            send_sem=halo_send,
            recv_sem=halo_recv.at[way, k],
            device_id=place_of(after + way * (before - after)),
            device_id_type=MESH,
        )

    patient = slab == (1 - quick) + quick * (total - 2)
    for k in range(STEPS):
        for way, r in ((0, rows - 1 - k), (1, k)):
            row_load(r).wait()
            edges[way, k] = lev[STEPS + r].astype(jnp.bfloat16)
        if k == 0:
            pl.semaphore_wait(barrier, len(targets))

        @pl.when(jnp.logical_not(patient))
        def _():
            halo_copy(quick, k).start()

        halo_copy(1 - quick, k).start()

    def stencil(base, half):
        def at(i):
            return [lev[i, f, pl.ds(half, 8), :] for f in range(fields)]

        return advance(at(base - 1), at(base), at(base + 1))

    def step_row(level, line):
        base = level * lines + line
        for m in range(0, ens, 8):
            done = stencil(base, m)
            for f in range(fields):
                lev[base + lines, f, pl.ds(m, 8), :] = done[f]

    for level in range(STEPS - 1):

        def inner_row(i, carry, level=level):
            step_row(level, STEPS + level + 1 + i)
            return carry

        lax.fori_loop(0, rows - 2 * (level + 1), inner_row, 0)
        if level == 0:
            @pl.when(patient)
            def _():
                for k in range(STEPS):
                    halo_copy(quick, k).start()


    def wave_side(w):
        late = w // STEPS
        return quick + late - 2 * quick * late, lax.rem(w, STEPS)

    def wave_row(w):
        side, k = wave_side(w)
        return (STEPS - 1 - k) + side * (2 * k + 1)

    def span(w, kind):
        return pl.ds(*((0, fields), (0, 1), (1, fields - 1))[kind]), part_recv.at[w + kind // 2 * LAST]

    def part_start(w, kind):
        here, landed = span(w, kind)
        for peer in peers:
            pltpu.make_async_remote_copy(
                src_ref=ready.at[w, peer, here],
                dst_ref=recv.at[w, here, pl.ds(me * ens, ens)],
                send_sem=part_send,
                recv_sem=landed,
                device_id={"mem": peer},
                device_id_type=MESH,
            ).start()
        pltpu.make_async_copy(ready.at[w, me, here], recv.at[w, here, pl.ds(me * ens, ens)], landed).start()

    def arrived(w, kind):
        here, landed = span(w, kind)
        pltpu.make_async_copy(recv.at[w, here], recv.at[w, here], landed).wait()

    def place(w):
        side, k = wave_side(w)
        return side, k, 1 - 2 * side, (STEPS - 1 - k) + side * (2 * k + lines - 2 * STEPS + 1)

    def make_ready(w, m, pair):
        for f in range(fields):
            both = jnp.concatenate([pair[0][f], pair[1][f]], axis=0).astype(jnp.bfloat16)
            for d in range(parts):
                ready[w, d, f, pl.ds(m, 16), :] = both[:, d * tile_cols : (d + 1) * tile_cols]

    def wave(w, carry):
        side, k, sign, start = place(w)
        halo_copy(side, k).wait_recv()
        lev[start] = halo[side, k].astype(jnp.float32)

        def up(level, c):
            step_row(level, start + sign * (level + 1))
            return c

        lax.fori_loop(0, STEPS - 1, up, 0)
        base = (STEPS - 1) * lines + start + sign * STEPS
        for m in range(0, ens, 16):
            make_ready(w, m, [stencil(base, m), stencil(base, m + 8)])
        part_start(w, 0)
        return carry

    def late_wave(w, kind, last=False):
        side, k, sign, start = place(w)
        toward = courant * sign.astype(jnp.float32)

        def prepare(level, c):
            base = level * lines + start + sign * (level + 1)
            for m in range(0, ens, 8):
                mid, far = ([lev[i, f, pl.ds(m, 8), :] for f in range(fields)] for i in (base, base + sign))
                for i, q in enumerate(known(mid, far, toward)):
                    partial[level, i, pl.ds(m, 8), :] = q
            return c

        lax.fori_loop(0, STEPS, prepare, 0)
        halo_copy(side, k).wait_recv()
        for m in range(0, ens, 16):
            rows16 = [halo[side, k, f, pl.ds(m, 16), :].astype(jnp.float32) for f in range(fields)]
            pair = []
            for half in range(2):
                now = [q[8 * half : 8 * half + 8] for q in rows16]
                here = pl.ds(m + 8 * half, 8)
                for level in range(STEPS):
                    if not last:
                        for f in range(fields):
                            lev[level * lines + start + sign * level, f, here, :] = now[f]
                    now = joined(now, [partial[level, i, here, :] for i in range(fields + 1)], toward)
                pair.append(now)
            make_ready(w, m, pair)
        part_start(w, kind)

    def late_loop(w, carry):
        late_wave(w, 0)
        return carry

    lax.fori_loop(0, STEPS, wave, 0)

    lax.fori_loop(STEPS, waves - LAST, late_loop, 0)
    for w in range(waves - LAST, waves):
        late_wave(w, 1, w == waves - 1)
    for w in range(waves - LAST, waves):
        part_start(w, 2)

    for load in small:
        load.wait()

    def select(w, carry):
        ids = lax.broadcasted_iota(jnp.int32, (tile_cols, slots), 0) + wave_row(w) * tile_cols
        pick[pl.ds(pl.multiple_of(w * tile_cols, tile_cols), tile_cols), :] = jnp.where(
            ids == cells[...], 1.0, 0.0
        ).astype(jnp.bfloat16)
        return carry

    lax.fori_loop(0, waves, select, 0)
    slot_ids = lax.broadcasted_iota(jnp.int32, (1, slots), 1)
    weights = jnp.where(slot_ids < count[...], 1.0 / (error[...] * error[...]), 0.0)
    chunk = 256 if slots % 256 == 0 else slots
    for s in range(0, slots, chunk):
        cut = slice(s, s + chunk)
        asked = weights[:, cut] * (values[:, cut] + error[:, cut] * noise[cut, :].T)
        for i, third in enumerate(split(asked)[:2]):
            target[i * full : (i + 1) * full, cut] = third
    line_ids = lax.broadcasted_iota(jnp.int32, (16, slots), 0)
    thirds = [q.astype(jnp.float32) for q in split(weights)]
    target[2 * full :, :] = jnp.where(
        line_ids == 0, thirds[0], jnp.where(line_ids == 1, thirds[1], jnp.where(line_ids == 2, thirds[2], 0.0))
    ).astype(jnp.bfloat16)

    def turned(a, b):
        return lax.dot_general(a, b, (((1,), (1,)), ((), ())), preferred_element_type=jnp.float32)

    chunk = 2 * tile_cols
    for c in range(0, points, chunk):
        cut = slice(c, c + chunk)
        summed = turned(target[...], pick[cut, :])
        for i, third in enumerate(split(summed[:full] + summed[full : 2 * full])[:2]):
            wanted[i * full : (i + 1) * full, cut] = third
        tail = summed[2 * full :]
        heavy[:, cut] = tail[0:1] + (tail[1:2] + tail[2:3])

    def observe(first, number):
        cut = slice(first * tile_cols, (first + number) * tile_cols)
        seen = jnp.concatenate([recv[w, 0] for w in range(first, first + number)], axis=1)
        near = seen.astype(jnp.float32)
        spread = near - jnp.sum(near, axis=0, keepdims=True) * (1.0 / full)
        wh, wm, wl = split(spread * heavy[:, cut])
        one = turned(seen, jnp.concatenate([wh, wm], axis=0))
        plain = one[:, :full] + (one[:, full:] + turned(seen, wl))
        two = turned(wanted[:, cut], seen)
        return plain, two[:full] + two[full:]

    early = waves - 1
    for w in range(early):
        arrived(w, 1 if w >= waves - LAST else 0)
    plain, aimed = observe(0, early)
    arrived(early, 1)
    plain, aimed = (a + b for a, b in zip((plain, aimed), observe(early, 1)))
    least = full - 1.0
    eye = jnp.where(
        lax.broadcasted_iota(jnp.int32, (full, full), 0) == lax.broadcasted_iota(jnp.int32, (full, full), 1), 1.0, 0.0
    )
    gram = plain - jnp.sum(plain, axis=0, keepdims=True) * (1.0 / full) + least * eye
    rhs = aimed - plain
    rhs = rhs - jnp.sum(rhs, axis=1, keepdims=True) * (1.0 / full)
    solved, eye = solve_turned(gram, rhs, least)
    mix = solved + eye
    upper = mix.astype(jnp.bfloat16)
    lower = (mix - upper.astype(jnp.float32)).astype(jnp.bfloat16)
    mix = jnp.concatenate([upper, lower], axis=1)
    for f in range(fields):
        for w in range(0, waves, 2):
            if f == 1:
                for i in (w, w + 1):
                    if i >= waves - LAST:
                        arrived(i, 2)
            block = jnp.concatenate([recv[w, f], recv[w + 1, f]], axis=1)
            done = mxu(mix, jnp.concatenate([block, block], axis=0))
            for i in range(2):
                tall[f, pl.ds(wave_row(w + i), full, stride=rows), :] = done[:, i * tile_cols : (i + 1) * tile_cols]
        out[f] = tall[f].reshape(full, rows, tile_cols).astype(jnp.bfloat16)
    pltpu.make_async_copy(edges, edges, halo_send).wait()
    gone = ready.at[:, pl.ds(0, parts - 1)]
    pltpu.make_async_copy(gone, gone, part_send).wait()


def hbm():
    return pl.BlockSpec(memory_space=pltpu.HBM)


def stay(q):
    return pltpu.with_memory_space_constraint(q, pltpu.HBM)


def body(members, obs_cells, obs_count, obs_values, obs_error, obs_noise):
    fields, ens, rows, cols = members.shape
    parts = lax.axis_size("mem")
    tile_cols = cols // parts
    full = ens * parts
    points = rows * tile_cols
    slots = obs_cells.shape[2]
    lines = rows + 2 * STEPS
    edge = pltpu.VMEM((2, STEPS, fields, ens, cols), jnp.bfloat16)
    row = pltpu.VMEM((1, slots), jnp.float32)
    dma = pltpu.SemaphoreType.DMA
    return pl.pallas_call(
        kernel,
        name="assimilate",
        out_shape=jax.ShapeDtypeStruct((fields, full, rows, tile_cols), jnp.bfloat16),
        in_specs=[hbm()] * 6,
        out_specs=pl.BlockSpec(memory_space=pltpu.VMEM),
        scratch_shapes=[
            pltpu.VMEM((STEPS * lines, fields, ens, cols), jnp.float32),
            edge,
            edge,
            pltpu.VMEM((rows, parts, fields, ens, tile_cols), jnp.bfloat16),
            pltpu.VMEM((rows, fields, full, tile_cols), jnp.bfloat16),
            pltpu.VMEM((STEPS, fields + 1, ens, cols), jnp.float32),
            pltpu.VMEM(obs_noise.shape[2:], jnp.float32),
            pltpu.VMEM((1, slots), jnp.int32),
            row,
            row,
            pltpu.VMEM((1, 1), jnp.int32),
            pltpu.VMEM((points, slots), jnp.bfloat16),
            pltpu.VMEM((2 * full + 16, slots), jnp.bfloat16),
            pltpu.VMEM((2 * full, points), jnp.bfloat16),
            pltpu.VMEM((1, points), jnp.float32),
            pltpu.VMEM((fields, full * rows, tile_cols), jnp.float32),
            dma((rows,)),
            dma((5,)),
            dma,
            dma((2, STEPS)),
            dma,
            dma((rows + LAST,)),
        ],
        compiler_params=pltpu.CompilerParams(
            vmem_limit_bytes=VMEM_BYTES, collective_id=0, has_side_effects=True
        ),
    )(stay(members), obs_count, *[stay(q) for q in (obs_cells[0], obs_values[0], obs_error[0], obs_noise[0, 0])])


def solution(mesh):
    in_specs = (
        P(None, "mem", ("tile", "grp"), None),
        P(("tile", "grp"), "mem", None),
        P(("tile", "grp"), "mem"),
        P(("tile", "grp"), "mem", None),
        P(("tile", "grp"), "mem", None),
        P(("tile", "grp"), "mem", None, None),
    )
    out_specs = P(None, None, ("tile", "grp"), "mem")
    return jax.shard_map(body, mesh=mesh, in_specs=in_specs, out_specs=out_specs, check_vma=False)
```
